256 devices in a mesh: seq: 64 (over y, z, core), head: 4 (over x).
Axes of the slice: x: 4, y: 4, z: 8, core: 2. Of those that a mesh axis runs over, the one named last changes fastest.
Arguments:
- signal: bfloat16 [16384, 2048], P('seq', 'head'), may hold values from -6 to 6
- gate: bfloat16 [16384, 2048], P('seq', 'head'), may hold values from -6 to 6
- skip: float32 [2048], P('head'), may hold values from -4 to 4
- w_first: float32 [33, 64], replicated, may hold values from -1 to 1
- b_first: float32 [64], replicated, may hold values from -3.140625 to 3.140625
- freq: float32 [64], replicated, may hold values from 0.5 to 2
- w_mid: float32 [64, 64], replicated, may hold values from -0.75 to 0.75
- w_last: float32 [64, 2048], P(None, 'head'), may hold values from -0.046875 to 0.046875
- rate: float32 [2048], P('head'), may hold values from 0.00014648438 to 0.08
- out_w: bfloat16 [2048, 2048], P('head'), may hold values from -0.125 to 0.125
Outputs:
- output: bfloat16 [16384, 2048], P('seq', 'head')
The draws below stay inside these ranges and needn't reach their ends.
All inputs are finite; a program needn't handle non-finite values.
Results may differ from the reference program's by a relative error of at most 0.0054.
Values may be sent and summed in bfloat16 or wider, within the bound.
A program may use at most 64 MiB of HBM per device.

```python
import math
import jax
import jax.numpy as jnp
from jax import lax

D = 2048
K = 2048
FH = 64
BANDS = 16
E = 33
LENGTH = 16384


def draw_w_first(key, part):
    own_key = jax.random.fold_in(key, 101)
    return jax.random.uniform(own_key, (E, FH), jnp.float32, -1.0, 1.0)


def draw_w_mid(key, part):
    own_key = jax.random.fold_in(key, 202)
    return jax.random.uniform(own_key, (FH, FH), jnp.float32, -0.75, 0.75)


def block_scale(key, extent, cuts, low, high):
    level, own = 1.0, jax.random.fold_in(key, 6)
    for dim, blocks in cuts:
        heights = jnp.exp(jax.random.uniform(jax.random.fold_in(own, dim), (blocks,), jnp.float32, low / len(cuts), high / len(cuts)))
        level = level * jnp.repeat(heights, extent[dim] // blocks).reshape([-1 if axis == dim else 1 for axis in range(len(extent))])
    return level


def bell_draw(key, extent, deviation, reach, pieces=(), dtype=jnp.bfloat16):
    array = deviation * jax.random.normal(key, extent, jnp.float32)
    if pieces:
        array = array * block_scale(key, extent, pieces, -0.22, 0.18)
    return jnp.clip(array, -reach, reach).astype(dtype)


def setup_inputs(seed: int = 0) -> dict:
    streams_of = jax.random.split(jax.random.key(seed), 11)
    return {
        "signal": bell_draw(streams_of[0], (LENGTH, D), 1.0, 6.0, ((0, 64), (1, 4))),
        "gate": bell_draw(streams_of[1], (LENGTH, D), 1.0, 6.0, ((0, 64), (1, 4))),
        "skip": bell_draw(streams_of[2], (D,), 1.0, 4.0, ((0, 4),), jnp.float32),
        "w_first": draw_w_first(jax.random.fold_in(streams_of[10], 71), 0),
        "b_first": jnp.clip(jax.random.uniform(streams_of[4], (FH,), jnp.float32, -3.140625, 3.140625), -3.140625, 3.140625),
        "freq": jnp.clip(jax.random.uniform(streams_of[5], (FH,), jnp.float32, 0.5, 2.0), 0.5, 2.0),
        "w_mid": draw_w_mid(jax.random.fold_in(streams_of[10], 71), 0),
        "w_last": bell_draw(streams_of[7], (FH, D), (FH * 256) ** -0.5, 0.046875, ((1, 4),), jnp.float32),
        "rate": jnp.clip(jnp.exp(math.log(0.08) - 6.302863 * jax.random.uniform(streams_of[8], (D,), jnp.float32) ** block_scale(streams_of[8], (D,), ((0, 4),), -0.2, 0.2)), 0.00014648438, 0.08),
        "out_w": bell_draw(streams_of[9], (D, D), D ** -0.5, 0.125, ((0, 4),)),
    }


def make_filter(w_first, b_first, freq, w_mid, w_last, rate, start, count):
    highest = lax.Precision.HIGHEST
    position = (start + jnp.arange(count)).astype(jnp.float32)
    bands = jnp.arange(1, BANDS + 1).astype(jnp.float32)
    angles = 2.0 * math.pi * position[:, None] * bands[None, :] / K
    features = jnp.concatenate([position[:, None] / K, jnp.cos(angles), jnp.sin(angles)], 1)
    first = jnp.sin(freq * (jnp.dot(features, w_first, precision=highest) + b_first))
    second = jnp.sin(freq * jnp.dot(first, w_mid, precision=highest))
    raw = jnp.dot(second, w_last, precision=highest)
    return (raw * jnp.exp(-rate[None, :] * position[:, None])).astype(jnp.bfloat16)


def reference(signal, gate, skip, w_first, b_first, freq, w_mid, w_last, rate, out_w):
    filt = make_filter(w_first, b_first, freq, w_mid, w_last, rate, 0, K)
    size_fft = 1 << (LENGTH + K - 2).bit_length()
    blocks = D // 128
    values = signal.astype(jnp.float32).reshape(LENGTH, blocks, 128).transpose(1, 0, 2)
    kernels = filt.astype(jnp.float32).reshape(K, blocks, 128).transpose(1, 0, 2)

    def convolve(pair):
        left, right = pair
        product = jnp.fft.rfft(left, n=size_fft, axis=0) * jnp.fft.rfft(right, n=size_fft, axis=0)
        return jnp.fft.irfft(product, n=size_fft, axis=0)[:LENGTH]

    conv = lax.map(convolve, (values, kernels)).transpose(1, 0, 2).reshape(LENGTH, D)
    mixed = (gate.astype(jnp.float32) * (conv + skip[None, :] * signal.astype(jnp.float32))).astype(jnp.bfloat16)
    return jnp.dot(mixed, out_w, preferred_element_type=jnp.float32).astype(jnp.bfloat16)
```

```python
import functools
import math

import jax
import jax.numpy as jnp
import numpy as np
from jax import lax
from jax.experimental import pallas as pl
from jax.experimental.pallas import tpu as pltpu
from jax.sharding import PartitionSpec as P

K = 2048
BANDS = 16
LANES = 128
MESH = pl.DeviceIdType.MESH


def features():
    t = np.arange(K, dtype=np.float64)
    bands = np.arange(1, BANDS + 1, dtype=np.float64)
    angles = 2.0 * math.pi * t[None, :] * bands[:, None] / K
    rows = np.concatenate([t[None] / K, np.cos(angles), np.sin(angles), np.ones((1, K))], 0)
    rows = np.concatenate([rows, np.zeros((40 - rows.shape[0], K))], 0)
    return rows.astype(np.float32)


def sine(x):
    turns = jnp.round(x * (1.0 / math.pi))
    r = (x - turns * 3.140625) - turns * (math.pi - 3.140625)
    s = r * r
    p = -1.0 / 39916800.0
    for c in (1.0 / 362880.0, -1.0 / 5040.0, 1.0 / 120.0, -1.0 / 6.0):
        p = p * s + c
    v = r + r * s * p
    odd = jnp.bitwise_and(turns.astype(jnp.int32), 1)
    return jnp.where(odd == 1, -v, v)


def rows_of(tile, count):
    copies = jnp.broadcast_to(tile[None], (count // tile.shape[0], *tile.shape))
    return copies.reshape(count, tile.shape[1])


def dot_t(a, b):
    return lax.dot_general(
        a, b, (((0,), (0,)), ((), ())),
        precision=lax.Precision.HIGHEST, preferred_element_type=jnp.float32,
    )


def kernel(
    n, heads, sig_hbm, gate_hbm, skip_ref, wf_ref, bf_ref, freq_ref, wm_ref, wl_ref, rate_ref, w_hbm, feat_ref,
    out_ref,
    sig, gate, w, xsend, xrecv, xf, params, h_ref, skips, toep, yf, ysend, yrecv, mixed, part, psend, precv,
    in_sems, xs_sem, xr_sem, ys_sem, yr_sem, ps_sems, pr_sems,
):
    me = lax.axis_index("seq")
    hd = lax.axis_index("head")
    group = xsend.shape[1] // 2
    rows = sig.shape[0]
    width = sig.shape[1]

    loads = [
        pltpu.make_async_copy(sig_hbm, sig, in_sems.at[0]),
        pltpu.make_async_copy(gate_hbm, gate, in_sems.at[1]),
        pltpu.make_async_copy(w_hbm, w, in_sems.at[2]),
    ]
    for c in loads:
        c.start()

    barrier = pltpu.get_barrier_semaphore()

    def greet(k, carry):
        pl.semaphore_signal(barrier, inc=1, device_id={"seq": lax.rem(me + k, n)}, device_id_type=MESH)
        return carry

    lax.fori_loop(1, n, greet, 0)
    for k in range(1, heads):
        pl.semaphore_signal(barrier, inc=1, device_id={"head": lax.rem(hd + k, heads)}, device_id_type=MESH)

    loads[0].wait()
    xt = sig[...].astype(jnp.float32).T.reshape(n, group, rows)
    xsend[...] = jnp.concatenate([xt[:, :, :LANES], xt[:, :, LANES:]], 1).astype(jnp.bfloat16)

    pl.semaphore_wait(barrier, n - 1 + heads - 1)

    def send_x(k, carry):
        to = lax.rem(me + k, n)
        pltpu.make_async_remote_copy(
            src_ref=xsend.at[to], dst_ref=xrecv.at[me], send_sem=xs_sem, recv_sem=xr_sem,
            device_id={"seq": to}, device_id_type=MESH,
        ).start()
        return carry

    lax.fori_loop(1, n, send_x, 0)
    xrecv[pl.ds(me, 1)] = xsend[pl.ds(me, 1)]

    pad = jnp.zeros((LANES - wl_ref.shape[0] - 2, width), jnp.float32)
    stacked = jnp.concatenate([wl_ref[...], rate_ref[...], skip_ref[...], pad], 0)
    params[...] = stacked.T
    own = params[pl.ds(pl.multiple_of(me * group, group), group), :]
    hidden = wl_ref.shape[0]
    rate = own[:, hidden : hidden + 1]
    freq = freq_ref[...]
    wfb = jnp.concatenate(
        [wf_ref[...], bf_ref[...], jnp.zeros((40 - wf_ref.shape[0] - 1, hidden), jnp.float32)], 0
    ) * freq
    wm = wm_ref[...] * freq
    step = 512
    for j in range(K // step):
        cols = slice(j * step, (j + 1) * step)
        first = sine(dot_t(wfb, feat_ref[:, cols]))
        second = sine(dot_t(wm, first))
        raw = jnp.dot(
            own[:, :hidden], second, precision=lax.Precision.HIGHEST, preferred_element_type=jnp.float32
        )
        t = (lax.broadcasted_iota(jnp.int32, (group, step), 1) + j * step).astype(jnp.float32)
        taps_here = (raw * jnp.exp(-rate * t)).astype(jnp.bfloat16).astype(jnp.float32)
        h_ref[:, :, cols] = jnp.broadcast_to(taps_here[:, None], (group, 8, step))
    skip_col = jnp.broadcast_to(own[:, hidden + 1 : hidden + 2], (group, LANES))
    skips[...] = jnp.broadcast_to(skip_col[:, None], (group, 8, LANES))

    upper = lax.broadcasted_iota(jnp.int32, (LANES, LANES), 1) >= lax.broadcasted_iota(
        jnp.int32, (LANES, LANES), 0
    )
    taps = K // LANES

    def build(c, carry):
        last = jnp.zeros((LANES, LANES), jnp.float32)
        for m in range(taps + 1):
            if m < taps:
                line = rows_of(h_ref[c, :, m * LANES : (m + 1) * LANES], LANES)
                rolled = pltpu.roll(line, 0, 1, stride=1, stride_axis=0)
            else:
                rolled = jnp.zeros((LANES, LANES), jnp.float32)
            toep[c, m * LANES : (m + 1) * LANES, :] = jnp.where(upper, rolled, last).astype(jnp.bfloat16)
            last = rolled
        return carry

    lax.fori_loop(0, group, build, 0)

    every = pl.ds(0, n - 1)
    pltpu.make_async_remote_copy(
        src_ref=xsend.at[every], dst_ref=xrecv.at[every], send_sem=xs_sem, recv_sem=xr_sem,
        device_id={"seq": lax.rem(me + 1, n)}, device_id_type=MESH,
    ).wait()
    blocks = 2 * n
    front = taps * group
    xf[:front, :] = jnp.zeros((front, LANES), jnp.float32)
    xf[front:, :] = xrecv[...].astype(jnp.float32).reshape(blocks * group, LANES)

    def convolve(c, carry):
        pieces = [
            xf[pl.ds((taps - m) * group + c, blocks, stride=group), :] for m in range(taps + 1)
        ]
        lhs = jnp.concatenate([p.astype(jnp.bfloat16) for p in pieces], 1)
        y = jnp.dot(lhs, toep[c], preferred_element_type=jnp.float32)
        yf[pl.ds(c, blocks, stride=group), :] = y + rows_of(skips[c], blocks) * pieces[0]
        return carry

    lax.fori_loop(0, group, convolve, 0)
    ysend[...] = yf[...].reshape(n, 2 * group, LANES).astype(jnp.bfloat16)

    def send_y(k, carry):
        to = lax.rem(me + k, n)
        pltpu.make_async_remote_copy(
            src_ref=ysend.at[to], dst_ref=yrecv.at[me], send_sem=ys_sem, recv_sem=yr_sem,
            device_id={"seq": to}, device_id_type=MESH,
        ).start()
        return carry

    lax.fori_loop(1, n, send_y, 0)
    yrecv[pl.ds(me, 1)] = ysend[pl.ds(me, 1)]
    loads[1].wait()
    loads[2].wait()
    pltpu.make_async_remote_copy(
        src_ref=ysend.at[every], dst_ref=yrecv.at[every], send_sem=ys_sem, recv_sem=yr_sem,
        device_id={"seq": lax.rem(me + 1, n)}, device_id_type=MESH,
    ).wait()

    y = yrecv[...].astype(jnp.float32).reshape(n, 2, group, LANES)
    for r in range(2):
        here = slice(r * LANES, (r + 1) * LANES)
        v = y[:, r].reshape(n * group, LANES).T
        mixed[here, :] = (gate[here, :].astype(jnp.float32) * v).astype(jnp.bfloat16)

    copies = []
    for i, k in enumerate((2, 1, 3)):
        to = lax.rem(hd + k, heads)
        cols = pl.ds(pl.multiple_of(to * width, width), width)
        psend[i] = jnp.dot(mixed[...], w[:, cols], preferred_element_type=jnp.float32).astype(jnp.bfloat16)
        copy = pltpu.make_async_remote_copy(
            src_ref=psend.at[i], dst_ref=precv.at[i], send_sem=ps_sems.at[i], recv_sem=pr_sems.at[i],
            device_id={"head": to}, device_id_type=MESH,
        )
        copy.start()
        copies.append(copy)
    cols = pl.ds(pl.multiple_of(hd * width, width), width)
    part[...] = jnp.dot(mixed[...], w[:, cols], preferred_element_type=jnp.float32)
    for copy in copies:
        copy.wait()
    total = part[...]
    for i in range(heads - 1):
        total = total + precv[i].astype(jnp.float32)
    out_ref[...] = total.astype(jnp.bfloat16)


def local(signal, gate, skip, w_first, b_first, freq, w_mid, w_last, rate, out_w):
    n, heads = lax.axis_size("seq"), lax.axis_size("head")
    rows, width = signal.shape
    group = width // n
    bf16, f32 = jnp.bfloat16, jnp.float32
    vmem = pl.BlockSpec(memory_space=pltpu.VMEM)
    hbm = pl.BlockSpec(memory_space=pl.ANY)
    dma = pltpu.SemaphoreType.DMA
    return pl.pallas_call(
        functools.partial(kernel, n, heads),
        out_shape=jax.ShapeDtypeStruct((rows, width), bf16),
        in_specs=[hbm, hbm, vmem, vmem, vmem, vmem, vmem, vmem, vmem, hbm, vmem],
        out_specs=vmem,
        scratch_shapes=[
            pltpu.VMEM((rows, width), bf16),
            pltpu.VMEM((rows, width), bf16),
            pltpu.VMEM(out_w.shape, bf16),
            pltpu.VMEM((n, 2 * group, LANES), bf16),
            pltpu.VMEM((n, 2 * group, LANES), bf16),
            pltpu.VMEM(((2 * n + K // LANES) * group, LANES), f32),
            pltpu.VMEM((width, LANES), f32),
            pltpu.VMEM((group, 8, K), f32),
            pltpu.VMEM((group, 8, LANES), f32),
            pltpu.VMEM((group, K + LANES, LANES), bf16),
            pltpu.VMEM((2 * n * group, LANES), f32),
            pltpu.VMEM((n, 2 * group, LANES), bf16),
            pltpu.VMEM((n, 2 * group, LANES), bf16),
            pltpu.VMEM((rows, width), bf16),
            pltpu.VMEM((rows, width), f32),
            pltpu.VMEM((heads - 1, rows, width), bf16),
            pltpu.VMEM((heads - 1, rows, width), bf16),
            dma((3,)), dma, dma, dma, dma, dma((heads - 1,)), dma((heads - 1,)),
        ],
        compiler_params=pltpu.CompilerParams(collective_id=0, has_side_effects=True),
    )(
        signal, gate, skip[None], w_first, b_first[None], freq[None], w_mid, w_last, rate[None], out_w,
        jnp.asarray(features()),
    )


def solution(mesh):
    placed = (
        P("seq", "head"),
        P("seq", "head"),
        P("head"),
        P(),
        P(),
        P(),
        P(),
        P(None, "head"),
        P("head"),
        P("head", None),
    )
    return jax.shard_map(
        local, mesh=mesh, in_specs=placed, out_specs=P("seq", "head"), check_vma=False
    )
```

```python
import functools
import math

import jax
import jax.numpy as jnp
import numpy as np
from jax import lax
from jax.experimental import pallas as pl
from jax.experimental.pallas import tpu as pltpu
from jax.sharding import PartitionSpec as P

K = 2048
BANDS = 16
LANES = 128
ZS = 8
MESH = pl.DeviceIdType.MESH


def features():
    t = np.arange(K, dtype=np.float64)
    bands = np.arange(1, BANDS + 1, dtype=np.float64)
    angles = 2.0 * math.pi * t[None, :] * bands[:, None] / K
    rows = np.concatenate([t[None] / K, np.cos(angles), np.sin(angles), np.ones((1, K))], 0)
    rows = np.concatenate([rows, np.zeros((40 - rows.shape[0], K))], 0)
    return rows.astype(np.float32)


def sine(x):
    turns = jnp.round(x * (1.0 / math.pi))
    r = (x - turns * 3.140625) - turns * (math.pi - 3.140625)
    s = r * r
    p = -1.0 / 39916800.0
    for c in (1.0 / 362880.0, -1.0 / 5040.0, 1.0 / 120.0, -1.0 / 6.0):
        p = p * s + c
    v = r + r * s * p
    odd = jnp.bitwise_and(turns.astype(jnp.int32), 1)
    return jnp.where(odd == 1, -v, v)


def rows_of(tile, count):
    copies = jnp.broadcast_to(tile[None], (count // tile.shape[0], *tile.shape))
    return copies.reshape(count, tile.shape[1])


def dot_t(a, b):
    return lax.dot_general(
        a, b, (((0,), (0,)), ((), ())),
        precision=lax.Precision.HIGHEST, preferred_element_type=jnp.float32,
    )


def kernel(
    n, heads, sig_hbm, gate_hbm, skip_ref, wf_ref, bf_ref, freq_ref, wm_ref, wl_ref, rate_ref, w_hbm, feat_ref,
    out_ref,
    sig, gate, wc, xsend, xrecv, xf, params, h_ref, skips, toep, yf, ysend, yrecv, mixed, part,
    in_sems, xs_sem, xr_sem, ys_sem, yr_sems, ws_sems, wr_sems, fs_sems, fr_sems, gs_sems, gr_sems,
):
    me = lax.axis_index("seq")
    hd = lax.axis_index("head")
    group = xsend.shape[1] // 2
    rows, width = sig.shape
    pairs = width // LANES
    per_pair = n // pairs

    y, z, core = me // (2 * ZS), lax.rem(me // 2, ZS), lax.rem(me, 2)
    ys = n // (2 * ZS)
    pair = z // 2
    own_group = z * (2 * ys) + y * 2 + core

    def peer(q, k):
        pz = lax.rem(pair + q, pairs) * 2 + lax.rem(z + k // (2 * ys), 2)
        py = lax.rem(y + lax.rem(k // 2, ys), ys)
        pc = lax.rem(core + k, 2)
        return py * (2 * ZS) + pz * 2 + pc, pz * (2 * ys) + py * 2 + pc

    cols = pl.ds(pl.multiple_of(hd * width, width), width)
    loads = [
        pltpu.make_async_copy(sig_hbm, sig, in_sems.at[0]),
        pltpu.make_async_copy(gate_hbm, gate, in_sems.at[1]),
        pltpu.make_async_copy(w_hbm.at[:, cols], wc.at[hd], in_sems.at[2]),
    ]
    for c in loads:
        c.start()

    barrier = pltpu.get_barrier_semaphore()

    def greet(k, carry):
        pl.semaphore_signal(barrier, inc=1, device_id={"seq": lax.rem(me + k, n)}, device_id_type=MESH)
        return carry

    lax.fori_loop(1, n, greet, 0)
    for k in range(1, heads):
        pl.semaphore_signal(barrier, inc=1, device_id={"head": lax.rem(hd + k, heads)}, device_id_type=MESH)

    loads[0].wait()
    xt = sig[...].astype(jnp.float32).T.reshape(n, group, rows)
    xsend[...] = jnp.concatenate([xt[:, :, :LANES], xt[:, :, LANES:]], 1).astype(jnp.bfloat16)

    pl.semaphore_wait(barrier, n - 1 + heads - 1)

    for q in (2, 1, 3, 0):

        def send_x(k, carry, q=q):
            to, slot = peer(q, k)
            pltpu.make_async_remote_copy(
                src_ref=xsend.at[slot], dst_ref=xrecv.at[me], send_sem=xs_sem, recv_sem=xr_sem,
                device_id={"seq": to}, device_id_type=MESH,
            ).start()
            return carry

        lax.fori_loop(0 if q else 1, per_pair, send_x, 0)
    xrecv[pl.ds(me, 1)] = xsend[pl.ds(own_group, 1)]

    half = pl.ds(pl.multiple_of(core * (width // 2), width // 2), width // 2)
    fetches = []
    for i, k in enumerate((2, 1, 3)):
        to = lax.rem(hd + k, heads)
        there = pl.ds(pl.multiple_of(to * width, width), width)
        fetch = pltpu.make_async_remote_copy(
            src_ref=w_hbm.at[half, there], dst_ref=wc.at[hd, half], send_sem=ws_sems.at[i],
            recv_sem=wr_sems.at[i], device_id={"head": to}, device_id_type=MESH,
        )
        fetch.start()
        fetches.append(fetch)

    pad = jnp.zeros((LANES - wl_ref.shape[0] - 2, width), jnp.float32)
    stacked = jnp.concatenate([wl_ref[...], rate_ref[...], skip_ref[...], pad], 0)
    params[...] = stacked.T
    own = params[pl.ds(pl.multiple_of(own_group * group, group), group), :]
    hidden = wl_ref.shape[0]
    rate = own[:, hidden : hidden + 1]
    freq = freq_ref[...]
    wfb = jnp.concatenate(
        [wf_ref[...], bf_ref[...], jnp.zeros((40 - wf_ref.shape[0] - 1, hidden), jnp.float32)], 0
    ) * freq
    wm = wm_ref[...] * freq
    step = 512
    for j in range(K // step):
        here = slice(j * step, (j + 1) * step)
        first = sine(dot_t(wfb, feat_ref[:, here]))
        second = sine(dot_t(wm, first))
        raw = jnp.dot(
            own[:, :hidden], second, precision=lax.Precision.HIGHEST, preferred_element_type=jnp.float32
        )
        t = (lax.broadcasted_iota(jnp.int32, (group, step), 1) + j * step).astype(jnp.float32)
        taps_here = (raw * jnp.exp(-rate * t)).astype(jnp.bfloat16).astype(jnp.float32)
        h_ref[:, :, here] = jnp.broadcast_to(taps_here[:, None], (group, 8, step))
    skip_col = jnp.broadcast_to(own[:, hidden + 1 : hidden + 2], (group, LANES))
    skips[...] = jnp.broadcast_to(skip_col[:, None], (group, 8, LANES))

    upper = lax.broadcasted_iota(jnp.int32, (LANES, LANES), 1) >= lax.broadcasted_iota(
        jnp.int32, (LANES, LANES), 0
    )
    taps = K // LANES

    def build(c, carry):
        last = jnp.zeros((LANES, LANES), jnp.float32)
        for m in range(taps + 1):
            if m < taps:
                line = rows_of(h_ref[c, :, m * LANES : (m + 1) * LANES], LANES)
                rolled = pltpu.roll(line, 0, 1, stride=1, stride_axis=0)
            else:
                rolled = jnp.zeros((LANES, LANES), jnp.float32)
            toep[c, m * LANES : (m + 1) * LANES, :] = jnp.where(upper, rolled, last).astype(jnp.bfloat16)
            last = rolled
        return carry

    lax.fori_loop(0, group, build, 0)

    every = pl.ds(0, n - 1)
    pltpu.make_async_remote_copy(
        src_ref=xsend.at[every], dst_ref=xrecv.at[every], send_sem=xs_sem, recv_sem=xr_sem,
        device_id={"seq": lax.rem(me + 1, n)}, device_id_type=MESH,
    ).wait()
    blocks = 2 * n
    front = taps * group
    xf[:front, :] = jnp.zeros((front, LANES), jnp.float32)
    xf[front:, :] = xrecv[...].astype(jnp.float32).reshape(blocks * group, LANES)

    def convolve(c, carry):
        pieces = [
            xf[pl.ds((taps - m) * group + c, blocks, stride=group), :] for m in range(taps + 1)
        ]
        lhs = jnp.concatenate([p.astype(jnp.bfloat16) for p in pieces], 1)
        conv = jnp.dot(lhs, toep[c], preferred_element_type=jnp.float32)
        yf[pl.ds(c, blocks, stride=group), :] = conv + rows_of(skips[c], blocks) * pieces[0]
        return carry

    lax.fori_loop(0, group, convolve, 0)
    ysend[...] = yf[...].reshape(n, 2 * group, LANES).astype(jnp.bfloat16)

    order = (0, 1, 3, 2)
    for q in order:

        def send_y(k, carry, q=q):
            to, slot = peer(q, k)
            pltpu.make_async_remote_copy(
                src_ref=ysend.at[to], dst_ref=yrecv.at[own_group], send_sem=ys_sem, recv_sem=yr_sems.at[pair],
                device_id={"seq": to}, device_id_type=MESH,
            ).start()
            return carry

        lax.fori_loop(0 if q else 1, per_pair, send_y, 0)
    yrecv[pl.ds(own_group, 1)] = ysend[pl.ds(me, 1)]

    partner = me + 1 - 2 * core
    passes = []
    for i, k in enumerate((2, 1, 3)):
        fetches[i].wait()
        whose = lax.rem(hd + heads - k, heads)
        onward = pltpu.make_async_remote_copy(
            src_ref=wc.at[whose, half], dst_ref=wc.at[whose, half], send_sem=fs_sems.at[i],
            recv_sem=fr_sems.at[i], device_id={"seq": partner}, device_id_type=MESH,
        )
        onward.start()
        passes.append(onward)
    loads[1].wait()
    loads[2].wait()

    right, left = lax.rem(hd + 1, heads), lax.rem(hd + heads - 1, heads)
    top, low = pl.ds(0, rows // 2), pl.ds(rows // 2, rows // 2)

    def hop(kind, b, ref, to):
        return pltpu.make_async_remote_copy(
            src_ref=ref, dst_ref=ref, send_sem=gs_sems.at[kind, b], recv_sem=gr_sems.at[kind, b],
            device_id={"head": to}, device_id_type=MESH,
        )

    started = []

    def onwards(b):
        p = lax.rem(pair + order[b], pairs)
        firsts[b][0].wait_recv()
        started.append(hop(2, b, mixed.at[left, p, top], right))
        started[-1].start()
        firsts[b][1].wait_recv()
        started.append(hop(3, b, mixed.at[right, p, low], left))
        started[-1].start()

    firsts = []
    for b, q in enumerate(order):
        p = lax.rem(pair + q, pairs)
        count = per_pair if q else per_pair - 1
        some = pl.ds(0, count)
        pltpu.make_async_remote_copy(
            src_ref=ysend.at[some], dst_ref=yrecv.at[some], send_sem=ys_sem, recv_sem=yr_sems.at[p],
            device_id={"seq": partner}, device_id_type=MESH,
        ).wait_recv()
        v = yrecv[pl.ds(pl.multiple_of(p * per_pair, per_pair), per_pair)].astype(jnp.float32)
        v = v.reshape(per_pair, 2, group, LANES)
        channels = pl.ds(pl.multiple_of(p * LANES, LANES), LANES)
        for r in range(2):
            here = slice(r * LANES, (r + 1) * LANES)
            vt = v[:, r].reshape(LANES, LANES).T
            mixed[hd, p, here, :] = (gate[here, channels].astype(jnp.float32) * vt).astype(jnp.bfloat16)
        firsts.append([hop(0, b, mixed.at[hd, p], right), hop(1, b, mixed.at[hd, p], left)])
        for copy in firsts[b]:
            copy.start()
        if b:
            onwards(b - 1)

    def product(h):
        lhs = jnp.concatenate([mixed[h, p] for p in range(pairs)], 1)
        return jnp.dot(lhs, wc[h], preferred_element_type=jnp.float32)

    for onward in passes:
        onward.wait()
    part[...] = product(hd)
    onwards(pairs - 1)
    part[...] += product(left) + product(right)
    for copy in started:
        copy.wait()
    out_ref[...] = (part[...] + product(lax.rem(hd + 2, heads))).astype(jnp.bfloat16)
    for copies in firsts:
        for copy in copies:
            copy.wait_send()
    pltpu.make_async_remote_copy(
        src_ref=ysend.at[every], dst_ref=yrecv.at[every], send_sem=ys_sem, recv_sem=yr_sems.at[0],
        device_id={"seq": partner}, device_id_type=MESH,
    ).wait_send()


def local(signal, gate, skip, w_first, b_first, freq, w_mid, w_last, rate, out_w):
    n, heads = lax.axis_size("seq"), lax.axis_size("head")
    rows, width = signal.shape
    group = width // n
    bf16, f32 = jnp.bfloat16, jnp.float32
    vmem = pl.BlockSpec(memory_space=pltpu.VMEM)
    hbm = pl.BlockSpec(memory_space=pl.ANY)
    dma = pltpu.SemaphoreType.DMA
    return pl.pallas_call(
        functools.partial(kernel, n, heads),
        out_shape=jax.ShapeDtypeStruct((rows, width), bf16),
        in_specs=[hbm, hbm, vmem, vmem, vmem, vmem, vmem, vmem, vmem, hbm, vmem],
        out_specs=vmem,
        scratch_shapes=[
            pltpu.VMEM((rows, width), bf16),
            pltpu.VMEM((rows, width), bf16),
            pltpu.VMEM((heads, width, width), bf16),
            pltpu.VMEM((n, 2 * group, LANES), bf16),
            pltpu.VMEM((n, 2 * group, LANES), bf16),
            pltpu.VMEM(((2 * n + K // LANES) * group, LANES), f32),
            pltpu.VMEM((width, LANES), f32),
            pltpu.VMEM((group, 8, K), f32),
            pltpu.VMEM((group, 8, LANES), f32),
            pltpu.VMEM((group, K + LANES, LANES), bf16),
            pltpu.VMEM((2 * n * group, LANES), f32),
            pltpu.VMEM((n, 2 * group, LANES), bf16),
            pltpu.VMEM((n, 2 * group, LANES), bf16),
            pltpu.VMEM((heads, width // LANES, rows, LANES), bf16),
            pltpu.VMEM((rows, width), f32),
            dma((3,)), dma, dma, dma, dma((width // LANES,)), dma((heads - 1,)), dma((heads - 1,)),
            dma((heads - 1,)), dma((heads - 1,)), dma((4, width // LANES)), dma((4, width // LANES)),
        ],
        compiler_params=pltpu.CompilerParams(collective_id=0, has_side_effects=True),
    )(
        signal, gate, skip[None], w_first, b_first[None], freq[None], w_mid, w_last, rate[None], out_w,
        jnp.asarray(features()),
    )


def solution(mesh):
    placed = (
        P("seq", "head"),
        P("seq", "head"),
        P("head"),
        P(),
        P(),
        P(),
        P(),
        P(None, "head"),
        P("head"),
        P("head", None),
    )
    return jax.shard_map(
        local, mesh=mesh, in_specs=placed, out_specs=P("seq", "head"), check_vma=False
    )
```

```python
import functools
import math

import jax
import jax.numpy as jnp
import numpy as np
from jax import lax
from jax.experimental import pallas as pl
from jax.experimental.pallas import tpu as pltpu
from jax.sharding import PartitionSpec as P

K = 2048
BANDS = 16
LANES = 128
ZS = 8
MESH = pl.DeviceIdType.MESH


def features():
    t = np.arange(K, dtype=np.float64)
    bands = np.arange(1, BANDS + 1, dtype=np.float64)
    angles = 2.0 * math.pi * t[None, :] * bands[:, None] / K
    rows = np.concatenate([t[None] / K, np.cos(angles), np.sin(angles), np.ones((1, K))], 0)
    rows = np.concatenate([rows, np.zeros((40 - rows.shape[0], K))], 0)
    return rows.astype(np.float32)


def sine(x):
    turns = jnp.round(x * (1.0 / math.pi))
    r = (x - turns * 3.140625) - turns * (math.pi - 3.140625)
    s = r * r
    p = -1.0 / 39916800.0
    for c in (1.0 / 362880.0, -1.0 / 5040.0, 1.0 / 120.0, -1.0 / 6.0):
        p = p * s + c
    v = r + r * s * p
    odd = jnp.bitwise_and(turns.astype(jnp.int32), 1)
    return jnp.where(odd == 1, -v, v)


def rows_of(tile, count):
    copies = jnp.broadcast_to(tile[None], (count // tile.shape[0], *tile.shape))
    return copies.reshape(count, tile.shape[1])


def dot_t(a, b):
    return lax.dot_general(
        a, b, (((0,), (0,)), ((), ())),
        precision=lax.Precision.HIGHEST, preferred_element_type=jnp.float32,
    )


def swap_halves(one, two):
    upper = lax.broadcasted_iota(jnp.int32, one.shape, 1) < 4
    moved_one, moved_two = pltpu.roll(one, 4, 1), pltpu.roll(two, 4, 1)
    return jnp.where(upper, one, moved_two), jnp.where(upper, moved_one, two)


def kernel(
    n, heads, sig_hbm, gate_hbm, skip_hbm, wf_hbm, bf_hbm, freq_hbm, wm_hbm, wl_hbm, rate_hbm, w_hbm, feat_hbm,
    out_ref,
    sig, gate, skip_ref, wf_ref, bf_ref, freq_ref, wm_ref, wl_ref, rate_ref, feat_ref,
    wc, wrelay, xsend, xrecv, xf, params, h_ref, skips, toep, yf, ysend, yrecv, mixed, part,
    in_sems, xs_sems, xr_sems, ys_sems, yr_sems, ws_sems, wr_sems, fs_sems, fr_sems, gs_sems, gr_sems,
):
    me = lax.axis_index("seq")
    hd = lax.axis_index("head")
    rows, width = sig.shape
    group = width // n
    part_group = group // 2
    chunks = width // LANES
    per_chunk = n // 2
    taps = K // LANES
    blocks = 2 * n

    ys = n // (2 * ZS)
    y, z, core = me // (2 * ZS), lax.rem(me // 2, ZS), lax.rem(me, 2)
    z_half, z_low = z // 4, lax.rem(z, 4)
    own_group = z * (2 * ys) + y * 2 + core
    y_at = [lax.rem(y + i, ys) for i in range(ys)]
    core_at = [core, 1 - core]

    def peers(z_list, own_first):
        found = []
        for i, pz in enumerate(z_list):
            for dy in (2, 1, 3, 0):
                for dc in (1, 0):
                    if not (own_first and i == len(z_list) - 1 and dy == 0 and dc == 0):
                        found.append((
                            y_at[dy] * (2 * ZS) + pz * 2 + core_at[dc],
                            pz * (2 * ys) + y_at[dy] * 2 + core_at[dc],
                        ))
        return found

    everyone = peers([lax.rem(z + i, ZS) for i in (4, 3, 5, 2, 6, 1, 7, 0)], True)
    near = peers([z_half * 4 + lax.rem(z_low + i, 4) for i in (2, 1, 3, 0)], True)
    far = peers([(1 - z_half) * 4 + lax.rem(z_low + i, 4) for i in (0, 1, 3, 2)], False)

    barrier = pltpu.get_barrier_semaphore()
    load_sig = pltpu.make_async_copy(sig_hbm, sig, in_sems.at[0])
    load_sig.start()
    for to, _ in everyone:
        pl.semaphore_signal(barrier, inc=1, device_id={"seq": to}, device_id_type=MESH)
    right, left, opp = lax.rem(hd + 1, heads), lax.rem(hd + heads - 1, heads), lax.rem(hd + 2, heads)
    for to in (opp, right, left):
        pl.semaphore_signal(barrier, inc=1, device_id={"head": to}, device_id_type=MESH)

    def columns(h):
        return pl.ds(pl.multiple_of(h * width, width), width)

    small = (
        (wf_hbm, wf_ref), (bf_hbm, bf_ref), (freq_hbm, freq_ref), (wm_hbm, wm_ref), (wl_hbm, wl_ref),
        (rate_hbm, rate_ref), (skip_hbm, skip_ref), (feat_hbm, feat_ref),
        (gate_hbm, gate), (w_hbm.at[:, columns(hd)], wc.at[hd]),
    )
    loads = [pltpu.make_async_copy(src, dst, in_sems.at[i + 1]) for i, (src, dst) in enumerate(small)]
    for load in loads:
        load.start()

    load_sig.wait()
    xt = sig[...].astype(jnp.float32).T
    for h in range(2):
        piece = xt[h * (width // 2) : (h + 1) * (width // 2)].reshape(n // 2, 8, rows)
        one, two = swap_halves(piece[:, :, :LANES], piece[:, :, LANES:])
        xsend[h] = jnp.stack([one, two], 1).reshape(n, 8, LANES).astype(jnp.bfloat16)

    pl.semaphore_wait(barrier, n - 1 + heads - 1)

    for h in range(2):
        for to, slot in everyone:
            pltpu.make_async_remote_copy(
                src_ref=xsend.at[h, slot], dst_ref=xrecv.at[h, me], send_sem=xs_sems.at[h],
                recv_sem=xr_sems.at[h], device_id={"seq": to}, device_id_type=MESH,
            ).start()
    for h in range(2):
        xrecv[h, pl.ds(me, 1)] = xsend[h, pl.ds(own_group, 1)]

    half = pl.ds(pl.multiple_of(core * (width // 2), width // 2), width // 2)
    quarters = [
        pl.ds(pl.multiple_of(core * (width // 2) + i * (width // 4), width // 4), width // 4) for i in range(2)
    ]

    def fetch(i, src, dst, to):
        return pltpu.make_async_remote_copy(
            src_ref=src, dst_ref=dst, send_sem=ws_sems.at[i], recv_sem=wr_sems.at[i],
            device_id={"head": to}, device_id_type=MESH,
        )

    fetches = [
        fetch(0, w_hbm.at[quarters[0], columns(opp)], wrelay.at[0], right),
        fetch(1, w_hbm.at[quarters[1], columns(opp)], wrelay.at[1], left),
        fetch(2, w_hbm.at[half, columns(right)], wc.at[hd, half], right),
        fetch(3, w_hbm.at[half, columns(left)], wc.at[hd, half], left),
        fetch(4, wrelay.at[0], wc.at[left, quarters[0]], right),
        fetch(5, wrelay.at[1], wc.at[right, quarters[1]], left),
    ]
    for i in range(4):
        fetches[i].start()

    for load in loads[:8]:
        load.wait()
    pad = jnp.zeros((LANES - wl_ref.shape[0] - 2, width), jnp.float32)
    stacked = jnp.concatenate([wl_ref[...], rate_ref[...], skip_ref[...], pad], 0)
    params[...] = stacked.T
    pair = own_group - core
    lower, upper = [
        params[pl.ds(pl.multiple_of(pair * part_group + h * (width // 2), 8), 8), :] for h in range(2)
    ]
    first_rows = lax.broadcasted_iota(jnp.int32, (8, LANES), 0) < 4
    even = jnp.where(first_rows, lower, pltpu.roll(upper, 4, 0))
    odd = jnp.where(first_rows, pltpu.roll(lower, 4, 0), upper)
    own = jnp.where(core == 0, even, odd)
    hidden = wl_ref.shape[0]
    rate = own[:, hidden : hidden + 1]
    freq = freq_ref[...]
    wfb = jnp.concatenate(
        [wf_ref[...], bf_ref[...], jnp.zeros((40 - wf_ref.shape[0] - 1, hidden), jnp.float32)], 0
    ) * freq
    wm = wm_ref[...] * freq
    step = 512
    for j in range(K // step):
        here = slice(j * step, (j + 1) * step)
        first = sine(dot_t(wfb, feat_ref[:, here]))
        second = sine(dot_t(wm, first))
        raw = jnp.dot(
            own[:, :hidden], second, precision=lax.Precision.HIGHEST, preferred_element_type=jnp.float32
        )
        t = (lax.broadcasted_iota(jnp.int32, (group, step), 1) + j * step).astype(jnp.float32)
        taps_here = (raw * jnp.exp(-rate * t)).astype(jnp.bfloat16).astype(jnp.float32)
        h_ref[:, :, here] = jnp.broadcast_to(taps_here[:, None], (group, 8, step))
    skip_col = jnp.broadcast_to(own[:, hidden + 1 : hidden + 2], (group, LANES))
    skips[...] = jnp.broadcast_to(skip_col[:, None], (group, 8, LANES))

    causal = lax.broadcasted_iota(jnp.int32, (LANES, LANES), 1) >= lax.broadcasted_iota(
        jnp.int32, (LANES, LANES), 0
    )

    def build(c, carry):
        last = jnp.zeros((LANES, LANES), jnp.float32)
        for m in range(taps + 1):
            if m < taps:
                line = rows_of(h_ref[c, :, m * LANES : (m + 1) * LANES], LANES)
                rolled = pltpu.roll(line, 0, 1, stride=1, stride_axis=0)
            else:
                rolled = jnp.zeros((LANES, LANES), jnp.float32)
            toep[c, m * LANES : (m + 1) * LANES, :] = jnp.where(causal, rolled, last).astype(jnp.bfloat16)
            last = rolled
        return carry

    lax.fori_loop(0, group, build, 0)

    every = pl.ds(0, n - 1)
    front = taps * part_group
    partner = me + 1 - 2 * core

    def exchanged(h):
        return pltpu.make_async_remote_copy(
            src_ref=xsend.at[h, every], dst_ref=xrecv.at[h, every], send_sem=xs_sems.at[h],
            recv_sem=xr_sems.at[h], device_id={"seq": partner}, device_id_type=MESH,
        )

    for h in range(2):
        exchanged(h).wait_recv()
        xf[h, :front, :] = jnp.zeros((front, LANES), jnp.float32)
        xf[h, front:, :] = xrecv[h].astype(jnp.float32).reshape(blocks * part_group, LANES)

        def convolve(c, carry, h=h):
            pieces = [
                xf[h, pl.ds((taps - m) * part_group + c, blocks, stride=part_group), :] for m in range(taps + 1)
            ]
            lhs = jnp.concatenate([p.astype(jnp.bfloat16) for p in pieces], 1)
            channel = c + h * part_group
            conv = jnp.dot(lhs, toep[channel], preferred_element_type=jnp.float32)
            yf[h, pl.ds(c, blocks, stride=part_group), :] = conv + rows_of(skips[channel], blocks) * pieces[0]
            return carry

        lax.fori_loop(0, part_group, convolve, 0)
        ysend[h] = yf[h].reshape(n, 8, LANES).astype(jnp.bfloat16)
        for to, _ in near + far:
            pltpu.make_async_remote_copy(
                src_ref=ysend.at[h, to], dst_ref=yrecv.at[h, own_group], send_sem=ys_sems.at[h],
                recv_sem=yr_sems.at[h, z_half], device_id={"seq": to}, device_id_type=MESH,
            ).start()
        yrecv[h, pl.ds(own_group, 1)] = ysend[h, pl.ds(me, 1)]

    for i in range(2):
        fetches[i].wait_recv()
        fetches[4 + i].start()

    def onward(i, ref):
        return pltpu.make_async_remote_copy(
            src_ref=ref, dst_ref=ref, send_sem=fs_sems.at[i], recv_sem=fr_sems.at[i],
            device_id={"seq": partner}, device_id_type=MESH,
        )

    passes = [onward(0, wc.at[left, half]), onward(1, wc.at[right, half]), onward(2, wc.at[opp, half])]
    loads[8].wait()

    top, low = pl.ds(0, rows // 2), pl.ds(rows // 2, rows // 2)

    def hop(kind, b, ref, to):
        return pltpu.make_async_remote_copy(
            src_ref=ref, dst_ref=ref, send_sem=gs_sems.at[kind, b], recv_sem=gr_sems.at[kind, b],
            device_id={"head": to}, device_id_type=MESH,
        )

    order = [(h, z_half if g == 0 else 1 - z_half, g) for h in range(2) for g in range(2)]
    firsts, seconds = [], []

    def onwards(b):
        p = order[b][0] * 2 + order[b][1]
        firsts[b][0].wait_recv()
        seconds.append(hop(2, b, mixed.at[left, p, top], right))
        seconds[-1].start()
        firsts[b][1].wait_recv()
        seconds.append(hop(3, b, mixed.at[right, p, low], left))
        seconds[-1].start()

    for b, (h, zs, g) in enumerate(order):
        p = h * 2 + zs
        some = pl.ds(0, per_chunk if g else per_chunk - 1)
        pltpu.make_async_remote_copy(
            src_ref=ysend.at[h, some], dst_ref=yrecv.at[h, some], send_sem=ys_sems.at[h],
            recv_sem=yr_sems.at[h, zs], device_id={"seq": partner}, device_id_type=MESH,
        ).wait_recv()
        v = yrecv[h, pl.ds(pl.multiple_of(zs * per_chunk, per_chunk), per_chunk)].astype(jnp.float32)
        v = v.reshape(per_chunk // 2, 2, 8, LANES)
        channels = pl.ds(pl.multiple_of(p * LANES, LANES), LANES)
        for r, piece in enumerate(swap_halves(v[:, 0], v[:, 1])):
            here = slice(r * LANES, (r + 1) * LANES)
            vt = piece.reshape(LANES, LANES).T
            mixed[hd, p, here, :] = (gate[here, channels].astype(jnp.float32) * vt).astype(jnp.bfloat16)
        firsts.append([hop(0, b, mixed.at[hd, p], right), hop(1, b, mixed.at[hd, p], left)])
        for copy in firsts[b]:
            copy.start()
        if b == 1:
            for i in range(2):
                fetches[2 + i].wait_recv()
                passes[i].start()
            onwards(0)

    def product(h):
        lhs = jnp.concatenate([mixed[h, p] for p in range(chunks)], 1)
        return jnp.dot(lhs, wc[h], preferred_element_type=jnp.float32)

    for i in range(2):
        fetches[4 + i].wait_recv()
    passes[2].start()
    loads[9].wait()
    onwards(1)
    part[...] = product(hd)
    onwards(2)
    onwards(3)
    for weights in passes:
        weights.wait_recv()
    part[...] += product(left) + product(right)
    for copy in seconds:
        copy.wait_recv()
    out_ref[...] = (part[...] + product(opp)).astype(jnp.bfloat16)

    for copies in (*firsts, seconds, passes, fetches):
        for copy in copies:
            copy.wait_send()
    for h in range(2):
        exchanged(h).wait_send()
        pltpu.make_async_remote_copy(
            src_ref=ysend.at[h, every], dst_ref=yrecv.at[h, every], send_sem=ys_sems.at[h],
            recv_sem=yr_sems.at[h, 0], device_id={"seq": partner}, device_id_type=MESH,
        ).wait_send()


def local(signal, gate, skip, w_first, b_first, freq, w_mid, w_last, rate, out_w):
    n, heads = lax.axis_size("seq"), lax.axis_size("head")
    rows, width = signal.shape
    group = width // n
    bf16, f32 = jnp.bfloat16, jnp.float32
    vmem = pl.BlockSpec(memory_space=pltpu.VMEM)
    hbm = pl.BlockSpec(memory_space=pl.ANY)
    dma = pltpu.SemaphoreType.DMA
    operands = (
        signal, gate, skip[None], w_first, b_first[None], freq[None], w_mid, w_last, rate[None], out_w,
        jnp.asarray(features()),
    )
    return pl.pallas_call(
        functools.partial(kernel, n, heads),
        out_shape=jax.ShapeDtypeStruct((rows, width), bf16),
        in_specs=[hbm] * 11,
        out_specs=vmem,
        scratch_shapes=[
            pltpu.VMEM((rows, width), bf16),
            pltpu.VMEM((rows, width), bf16),
            *[pltpu.VMEM(a.shape, a.dtype) for a in operands[2:9]],
            pltpu.VMEM(operands[10].shape, f32),
            pltpu.VMEM((heads, width, width), bf16),
            pltpu.VMEM((2, width // 4, width), bf16),
            pltpu.VMEM((2, n, group, LANES), bf16),
            pltpu.VMEM((2, n, group, LANES), bf16),
            pltpu.VMEM((2, (2 * n + K // LANES) * group // 2, LANES), f32),
            pltpu.VMEM((width, LANES), f32),
            pltpu.VMEM((group, 8, K), f32),
            pltpu.VMEM((group, 8, LANES), f32),
            pltpu.VMEM((group, K + LANES, LANES), bf16),
            pltpu.VMEM((2, n * group, LANES), f32),
            pltpu.VMEM((2, n, group, LANES), bf16),
            pltpu.VMEM((2, n, group, LANES), bf16),
            pltpu.VMEM((heads, width // LANES, rows, LANES), bf16),
            pltpu.VMEM((rows, width), f32),
            dma((11,)), dma((2,)), dma((2,)), dma((2,)), dma((2, 2)), dma((6,)), dma((6,)),
            dma((3,)), dma((3,)), dma((4, width // LANES)), dma((4, width // LANES)),
        ],
        compiler_params=pltpu.CompilerParams(collective_id=0, has_side_effects=True),
    )(*operands)


def solution(mesh):
    placed = (
        P("seq", "head"),
        P("seq", "head"),
        P("head"),
        P(),
        P(),
        P(),
        P(),
        P(None, "head"),
        P("head"),
        P("head", None),
    )
    return jax.shard_map(
        local, mesh=mesh, in_specs=placed, out_specs=P("seq", "head"), check_vma=False
    )
```

```python
import functools
import math

import jax
import jax.numpy as jnp
import numpy as np
from jax import lax
from jax.experimental import pallas as pl
from jax.experimental.pallas import tpu as pltpu
from jax.sharding import PartitionSpec as P

K = 2048
BANDS = 16
LANES = 128
ZS = 8
MESH = pl.DeviceIdType.MESH


def features():
    t = np.arange(K, dtype=np.float64)
    bands = np.arange(1, BANDS + 1, dtype=np.float64)
    angles = 2.0 * math.pi * t[None, :] * bands[:, None] / K
    rows = np.concatenate([t[None] / K, np.cos(angles), np.sin(angles), np.ones((1, K))], 0)
    rows = np.concatenate([rows, np.zeros((40 - rows.shape[0], K))], 0)
    return rows.astype(np.float32)


def sine(x):
    turns = jnp.round(x * (1.0 / math.pi))
    r = (x - turns * 3.140625) - turns * (math.pi - 3.140625)
    s = r * r
    p = -1.0 / 39916800.0
    for c in (1.0 / 362880.0, -1.0 / 5040.0, 1.0 / 120.0, -1.0 / 6.0):
        p = p * s + c
    v = r + r * s * p
    odd = jnp.bitwise_and(turns.astype(jnp.int32), 1)
    return jnp.where(odd == 1, -v, v)


def rows_of(tile, count):
    copies = jnp.broadcast_to(tile[None], (count // tile.shape[0], *tile.shape))
    return copies.reshape(count, tile.shape[1])


def dot_t(a, b):
    return lax.dot_general(
        a, b, (((0,), (0,)), ((), ())),
        precision=lax.Precision.HIGHEST, preferred_element_type=jnp.float32,
    )


def swap_halves(one, two):
    upper = lax.broadcasted_iota(jnp.int32, one.shape, 1) < 4
    moved_one, moved_two = pltpu.roll(one, 4, 1), pltpu.roll(two, 4, 1)
    return jnp.where(upper, one, moved_two), jnp.where(upper, moved_one, two)


def kernel(
    n, heads, sig_hbm, gate_hbm, skip_hbm, wf_hbm, bf_hbm, freq_hbm, wm_hbm, wl_hbm, rate_hbm, w_hbm, feat_hbm,
    out_ref,
    sig, gate, skip_ref, wf_ref, bf_ref, freq_ref, wm_ref, wl_ref, rate_ref, feat_ref,
    wc, wrelay, xsend, xrecv, xf, params, h_ref, skips, toep, yf, ysend, yrecv, mixed, part,
    in_sems, xs_sems, xr_sems, ys_sems, yr_sems, ws_sems, wr_sems, fs_sems, fr_sems, gs_sems, gr_sems,
):
    me = lax.axis_index("seq")
    hd = lax.axis_index("head")
    rows, width = sig.shape
    group = width // n
    part_group = group // 2
    chunks = width // LANES
    per_chunk = n // 2
    taps = K // LANES
    blocks = 2 * n

    ys = n // (2 * ZS)
    y, z, core = me // (2 * ZS), lax.rem(me // 2, ZS), lax.rem(me, 2)
    z_half, z_low = z // 4, lax.rem(z, 4)
    own_group = z * (2 * ys) + y * 2 + core
    y_at = [lax.rem(y + i, ys) for i in range(ys)]
    core_at = [core, 1 - core]

    def peers(z_list, own_first):
        found = []
        for i, pz in enumerate(z_list):
            for dy in (2, 1, 3, 0):
                for dc in (1, 0):
                    if not (own_first and i == len(z_list) - 1 and dy == 0 and dc == 0):
                        found.append((
                            y_at[dy] * (2 * ZS) + pz * 2 + core_at[dc],
                            pz * (2 * ys) + y_at[dy] * 2 + core_at[dc],
                        ))
        return found

    everyone = peers([lax.rem(z + i, ZS) for i in (4, 3, 5, 2, 6, 1, 7, 0)], True)
    near = peers([z_half * 4 + lax.rem(z_low + i, 4) for i in (2, 1, 3, 0)], True)
    far = peers([(1 - z_half) * 4 + lax.rem(z_low + i, 4) for i in (0, 1, 3, 2)], False)

    barrier = pltpu.get_barrier_semaphore()
    load_sig = pltpu.make_async_copy(sig_hbm, sig, in_sems.at[0])
    load_sig.start()
    for to, _ in everyone:
        pl.semaphore_signal(barrier, inc=1, device_id={"seq": to}, device_id_type=MESH)
    right, left, opp = lax.rem(hd + 1, heads), lax.rem(hd + heads - 1, heads), lax.rem(hd + 2, heads)
    for to in (opp, right, left):
        pl.semaphore_signal(barrier, inc=1, device_id={"head": to}, device_id_type=MESH)

    def columns(h):
        return pl.ds(pl.multiple_of(h * width, width), width)

    small = (
        (wf_hbm, wf_ref), (bf_hbm, bf_ref), (freq_hbm, freq_ref), (wm_hbm, wm_ref), (wl_hbm, wl_ref),
        (rate_hbm, rate_ref), (skip_hbm, skip_ref), (feat_hbm, feat_ref),
        (gate_hbm, gate), (w_hbm.at[:, columns(hd)], wc.at[hd]),
    )
    loads = [pltpu.make_async_copy(src, dst, in_sems.at[i + 1]) for i, (src, dst) in enumerate(small)]
    for load in loads:
        load.start()

    load_sig.wait()
    xt = sig[...].astype(jnp.float32).T
    for h in range(2):
        piece = xt[h * (width // 2) : (h + 1) * (width // 2)].reshape(n // 2, 8, rows)
        one, two = swap_halves(piece[:, :, :LANES], piece[:, :, LANES:])
        xsend[h] = jnp.stack([one, two], 1).reshape(n, 8, LANES).astype(jnp.bfloat16)

    pl.semaphore_wait(barrier, n - 1 + heads - 1)

    for h in range(2):
        for to, slot in everyone:
            pltpu.make_async_remote_copy(
                src_ref=xsend.at[h, slot], dst_ref=xrecv.at[h, me], send_sem=xs_sems.at[h],
                recv_sem=xr_sems.at[h], device_id={"seq": to}, device_id_type=MESH,
            ).start()
    for h in range(2):
        xrecv[h, pl.ds(me, 1)] = xsend[h, pl.ds(own_group, 1)]

    half = pl.ds(pl.multiple_of(core * (width // 2), width // 2), width // 2)
    quarters = [
        pl.ds(pl.multiple_of(core * (width // 2) + i * (width // 4), width // 4), width // 4) for i in range(2)
    ]

    def fetch(i, src, dst, to):
        return pltpu.make_async_remote_copy(
            src_ref=src, dst_ref=dst, send_sem=ws_sems.at[i], recv_sem=wr_sems.at[i],
            device_id={"head": to}, device_id_type=MESH,
        )

    fetches = [
        fetch(0, w_hbm.at[quarters[0], columns(opp)], wrelay.at[0], right),
        fetch(1, w_hbm.at[quarters[1], columns(opp)], wrelay.at[1], left),
        fetch(2, w_hbm.at[half, columns(right)], wc.at[hd, half], right),
        fetch(3, w_hbm.at[half, columns(left)], wc.at[hd, half], left),
        fetch(4, wrelay.at[0], wc.at[left, quarters[0]], right),
        fetch(5, wrelay.at[1], wc.at[right, quarters[1]], left),
    ]
    for i in range(4):
        fetches[i].start()

    for load in loads[:8]:
        load.wait()
    pad = jnp.zeros((LANES - wl_ref.shape[0] - 2, width), jnp.float32)
    stacked = jnp.concatenate([wl_ref[...], rate_ref[...], skip_ref[...], pad], 0)
    params[...] = stacked.T
    pair = own_group - core
    lower, upper = [
        params[pl.ds(pl.multiple_of(pair * part_group + h * (width // 2), 8), 8), :] for h in range(2)
    ]
    first_rows = lax.broadcasted_iota(jnp.int32, (8, LANES), 0) < 4
    even = jnp.where(first_rows, lower, pltpu.roll(upper, 4, 0))
    odd = jnp.where(first_rows, pltpu.roll(lower, 4, 0), upper)
    own = jnp.where(core == 0, even, odd)
    hidden = wl_ref.shape[0]
    rate = own[:, hidden : hidden + 1]
    freq = freq_ref[...]
    wfb = jnp.concatenate(
        [wf_ref[...], bf_ref[...], jnp.zeros((40 - wf_ref.shape[0] - 1, hidden), jnp.float32)], 0
    ) * freq
    wm = wm_ref[...] * freq
    step = 512
    for j in range(K // step):
        here = slice(j * step, (j + 1) * step)
        first = sine(dot_t(wfb, feat_ref[:, here]))
        second = sine(dot_t(wm, first))
        raw = jnp.dot(
            own[:, :hidden], second, precision=lax.Precision.HIGHEST, preferred_element_type=jnp.float32
        )
        t = (lax.broadcasted_iota(jnp.int32, (group, step), 1) + j * step).astype(jnp.float32)
        taps_here = (raw * jnp.exp(-rate * t)).astype(jnp.bfloat16).astype(jnp.float32)
        h_ref[:, :, here] = jnp.broadcast_to(taps_here[:, None], (group, 8, step))
    skip_col = jnp.broadcast_to(own[:, hidden + 1 : hidden + 2], (group, LANES))
    skips[...] = jnp.broadcast_to(skip_col[:, None], (group, 8, LANES))

    causal = lax.broadcasted_iota(jnp.int32, (LANES, LANES), 1) >= lax.broadcasted_iota(
        jnp.int32, (LANES, LANES), 0
    )

    def build(c, carry):
        last = jnp.zeros((LANES, LANES), jnp.float32)
        for m in range(taps + 1):
            if m < taps:
                line = rows_of(h_ref[c, :, m * LANES : (m + 1) * LANES], LANES)
                rolled = pltpu.roll(line, 0, 1, stride=1, stride_axis=0)
            else:
                rolled = jnp.zeros((LANES, LANES), jnp.float32)
            toep[c, m * LANES : (m + 1) * LANES, :] = jnp.where(causal, rolled, last).astype(jnp.bfloat16)
            last = rolled
        return carry

    lax.fori_loop(0, group, build, 0)

    every = pl.ds(0, n - 1)
    front = taps * part_group
    partner = me + 1 - 2 * core

    def exchanged(h):
        return pltpu.make_async_remote_copy(
            src_ref=xsend.at[h, every], dst_ref=xrecv.at[h, every], send_sem=xs_sems.at[h],
            recv_sem=xr_sems.at[h], device_id={"seq": partner}, device_id_type=MESH,
        )

    for h in range(2):
        exchanged(h).wait_recv()
        xf[h, :front, :] = jnp.zeros((front, LANES), jnp.float32)
        xf[h, front:, :] = xrecv[h].astype(jnp.float32).reshape(blocks * part_group, LANES)

        def convolve(c, carry, h=h):
            pieces = [
                xf[h, pl.ds((taps - m) * part_group + c, blocks, stride=part_group), :] for m in range(taps + 1)
            ]
            lhs = jnp.concatenate([p.astype(jnp.bfloat16) for p in pieces], 1)
            channel = c + h * part_group
            conv = jnp.dot(lhs, toep[channel], preferred_element_type=jnp.float32)
            yf[h, pl.ds(c, blocks, stride=part_group), :] = conv + rows_of(skips[channel], blocks) * pieces[0]
            return carry

        lax.fori_loop(0, part_group, convolve, 0)
        ysend[h] = yf[h].reshape(n, 8, LANES).astype(jnp.bfloat16)
        for to, _ in near + far:
            pltpu.make_async_remote_copy(
                src_ref=ysend.at[h, to], dst_ref=yrecv.at[h, own_group], send_sem=ys_sems.at[h],
                recv_sem=yr_sems.at[h, z_half], device_id={"seq": to}, device_id_type=MESH,
            ).start()
        yrecv[h, pl.ds(own_group, 1)] = ysend[h, pl.ds(me, 1)]

    for i in range(2):
        fetches[i].wait_recv()
        fetches[4 + i].start()

    def onward(i, ref):
        return pltpu.make_async_remote_copy(
            src_ref=ref, dst_ref=ref, send_sem=fs_sems.at[i], recv_sem=fr_sems.at[i],
            device_id={"seq": partner}, device_id_type=MESH,
        )

    passes = [onward(0, wc.at[left, half]), onward(1, wc.at[right, half]), onward(2, wc.at[opp, half])]
    loads[8].wait()

    top, low = pl.ds(0, rows // 2), pl.ds(rows // 2, rows // 2)

    def hop(kind, b, ref, to):
        return pltpu.make_async_remote_copy(
            src_ref=ref, dst_ref=ref, send_sem=gs_sems.at[kind, b], recv_sem=gr_sems.at[kind, b],
            device_id={"head": to}, device_id_type=MESH,
        )

    order = [(h, z_half if g == 0 else 1 - z_half, g) for h in range(2) for g in range(2)]
    chunk_of = [h * 2 + zs for h, zs, _ in order]
    firsts, seconds = [], []

    def onwards(b):
        p = chunk_of[b]
        firsts[b][0].wait_recv()
        seconds.append(hop(2, b, mixed.at[left, p, top], right))
        seconds[-1].start()
        firsts[b][1].wait_recv()
        seconds.append(hop(3, b, mixed.at[right, p, low], left))
        seconds[-1].start()

    for b, (h, zs, g) in enumerate(order):
        p = chunk_of[b]
        some = pl.ds(0, per_chunk if g else per_chunk - 1)
        pltpu.make_async_remote_copy(
            src_ref=ysend.at[h, some], dst_ref=yrecv.at[h, some], send_sem=ys_sems.at[h],
            recv_sem=yr_sems.at[h, zs], device_id={"seq": partner}, device_id_type=MESH,
        ).wait_recv()
        v = yrecv[h, pl.ds(pl.multiple_of(zs * per_chunk, per_chunk), per_chunk)].astype(jnp.float32)
        v = v.reshape(per_chunk // 2, 2, 8, LANES)
        channels = pl.ds(pl.multiple_of(p * LANES, LANES), LANES)
        for r, piece in enumerate(swap_halves(v[:, 0], v[:, 1])):
            here = slice(r * LANES, (r + 1) * LANES)
            vt = piece.reshape(LANES, LANES).T
            mixed[hd, p, here, :] = (gate[here, channels].astype(jnp.float32) * vt).astype(jnp.bfloat16)
        firsts.append([hop(0, b, mixed.at[hd, p], right), hop(1, b, mixed.at[hd, p], left)])
        if b == chunks - 1:
            firsts[b].append(hop(2, b, mixed.at[hd, p], opp))
        for copy in firsts[b]:
            copy.start()
        if b == 1:
            for i in range(2):
                fetches[2 + i].wait_recv()
                passes[i].start()
            onwards(0)

    def product_of_half(h, first):
        lhs = jnp.concatenate([mixed[h, first], mixed[h, first + 1]], 1)
        return jnp.dot(
            lhs, wc[h, first * LANES : (first + 2) * LANES], preferred_element_type=jnp.float32
        )

    for i in range(2):
        fetches[4 + i].wait_recv()
    passes[2].start()
    loads[9].wait()
    onwards(1)
    part[...] = product_of_half(hd, 0) + product_of_half(hd, 2)
    onwards(2)
    for weights in passes:
        weights.wait_recv()
    for b in range(2):
        for copy in seconds[2 * b : 2 * b + 2]:
            copy.wait_recv()
    part[...] += product_of_half(left, 0) + product_of_half(right, 0) + product_of_half(opp, 0)
    for copy in firsts[3][:2]:
        copy.wait_recv()
    part[...] += product_of_half(left, 2) + product_of_half(right, 2)
    for copy in (*seconds[4:], firsts[3][2]):
        copy.wait_recv()
    out_ref[...] = (part[...] + product_of_half(opp, 2)).astype(jnp.bfloat16)

    for copies in (*firsts, seconds, passes, fetches):
        for copy in copies:
            copy.wait_send()
    for h in range(2):
        exchanged(h).wait_send()
        pltpu.make_async_remote_copy(
            src_ref=ysend.at[h, every], dst_ref=yrecv.at[h, every], send_sem=ys_sems.at[h],
            recv_sem=yr_sems.at[h, 0], device_id={"seq": partner}, device_id_type=MESH,
        ).wait_send()


def local(signal, gate, skip, w_first, b_first, freq, w_mid, w_last, rate, out_w):
    n, heads = lax.axis_size("seq"), lax.axis_size("head")
    rows, width = signal.shape
    group = width // n
    bf16, f32 = jnp.bfloat16, jnp.float32
    vmem = pl.BlockSpec(memory_space=pltpu.VMEM)
    hbm = pl.BlockSpec(memory_space=pl.ANY)
    dma = pltpu.SemaphoreType.DMA
    operands = (
        signal, gate, skip[None], w_first, b_first[None], freq[None], w_mid, w_last, rate[None], out_w,
        jnp.asarray(features()),
    )
    return pl.pallas_call(
        functools.partial(kernel, n, heads),
        out_shape=pltpu.VMEM((rows, width), bf16),
        in_specs=[hbm] * 11,
        out_specs=vmem,
        scratch_shapes=[
            pltpu.VMEM((rows, width), bf16),
            pltpu.VMEM((rows, width), bf16),
            *[pltpu.VMEM(a.shape, a.dtype) for a in operands[2:9]],
            pltpu.VMEM(operands[10].shape, f32),
            pltpu.VMEM((heads, width, width), bf16),
            pltpu.VMEM((2, width // 4, width), bf16),
            pltpu.VMEM((2, n, group, LANES), bf16),
            pltpu.VMEM((2, n, group, LANES), bf16),
            pltpu.VMEM((2, (2 * n + K // LANES) * group // 2, LANES), f32),
            pltpu.VMEM((width, LANES), f32),
            pltpu.VMEM((group, 8, K), f32),
            pltpu.VMEM((group, 8, LANES), f32),
            pltpu.VMEM((group, K + LANES, LANES), bf16),
            pltpu.VMEM((2, n * group, LANES), f32),
            pltpu.VMEM((2, n, group, LANES), bf16),
            pltpu.VMEM((2, n, group, LANES), bf16),
            pltpu.VMEM((heads, width // LANES, rows, LANES), bf16),
            pltpu.VMEM((rows, width), f32),
            dma((11,)), dma((2,)), dma((2,)), dma((2,)), dma((2, 2)), dma((6,)), dma((6,)),
            dma((3,)), dma((3,)), dma((4, width // LANES)), dma((4, width // LANES)),
        ],
        compiler_params=pltpu.CompilerParams(collective_id=0, has_side_effects=True),
    )(*operands)


def solution(mesh):
    placed = (
        P("seq", "head"),
        P("seq", "head"),
        P("head"),
        P(),
        P(),
        P(),
        P(),
        P(None, "head"),
        P("head"),
        P("head", None),
    )
    return jax.shard_map(
        local, mesh=mesh, in_specs=placed, out_specs=P("seq", "head"), check_vma=False
    )
```

```python
import functools
import math

import jax
import jax.numpy as jnp
import numpy as np
from jax import lax
from jax.experimental import pallas as pl
from jax.experimental.pallas import tpu as pltpu
from jax.sharding import PartitionSpec as P

K = 2048
BANDS = 16
LANES = 128
ZS = 8
MESH = pl.DeviceIdType.MESH


def features():
    t = np.arange(K, dtype=np.float64)
    bands = np.arange(1, BANDS + 1, dtype=np.float64)
    angles = 2.0 * math.pi * t[None, :] * bands[:, None] / K
    rows = np.concatenate([t[None] / K, np.cos(angles), np.sin(angles), np.ones((1, K))], 0)
    rows = np.concatenate([rows, np.zeros((40 - rows.shape[0], K))], 0)
    return rows.astype(np.float32)


def sine(x):
    turns = jnp.round(x * (1.0 / math.pi))
    r = (x - turns * 3.140625) - turns * (math.pi - 3.140625)
    s = r * r
    p = -1.0 / 39916800.0
    for c in (1.0 / 362880.0, -1.0 / 5040.0, 1.0 / 120.0, -1.0 / 6.0):
        p = p * s + c
    v = r + r * s * p
    odd = jnp.bitwise_and(turns.astype(jnp.int32), 1)
    return jnp.where(odd == 1, -v, v)


def rows_of(tile, count):
    copies = jnp.broadcast_to(tile[None], (count // tile.shape[0], *tile.shape))
    return copies.reshape(count, tile.shape[1])


def dot_t(a, b):
    return lax.dot_general(
        a, b, (((0,), (0,)), ((), ())),
        precision=lax.Precision.HIGHEST, preferred_element_type=jnp.float32,
    )


def swap_halves(one, two):
    upper = lax.broadcasted_iota(jnp.int32, one.shape, 1) < 4
    moved_one, moved_two = pltpu.roll(one, 4, 1), pltpu.roll(two, 4, 1)
    return jnp.where(upper, one, moved_two), jnp.where(upper, moved_one, two)


def kernel(
    n, heads, sig_hbm, gate_hbm, skip_hbm, wf_hbm, bf_hbm, freq_hbm, wm_hbm, wl_hbm, rate_hbm, w_hbm, feat_hbm,
    out_ref,
    sig, gate, skip_ref, wf_ref, bf_ref, freq_ref, wm_ref, wl_ref, rate_ref, feat_ref,
    w_own, w_near, xsend, xrecv, xf, params, h_ref, skips, toep, yf, ysend, yrecv, mixed, part, psend, precv,
    in_sems, xs_sems, xr_sems, ys_sems, yr_sems, ws_sems, wr_sems, fs_sems, fr_sems, gs_sems, gr_sems, ps_sems, pr_sems,
):
    me = lax.axis_index("seq")
    hd = lax.axis_index("head")
    rows, width = sig.shape
    group = width // n
    part_group = group // 2
    per_chunk = n // 2
    taps = K // LANES
    blocks = 2 * n

    ys = n // (2 * ZS)
    y, z, core = me // (2 * ZS), lax.rem(me // 2, ZS), lax.rem(me, 2)
    z_half, z_low = z // 4, lax.rem(z, 4)
    own_group = z * (2 * ys) + y * 2 + core
    y_at = [lax.rem(y + i, ys) for i in range(ys)]
    core_at = [core, 1 - core]

    def peers(z_list, own_first):
        found = []
        for i, pz in enumerate(z_list):
            for dy in (2, 1, 3, 0):
                for dc in (1, 0):
                    if not (own_first and i == len(z_list) - 1 and dy == 0 and dc == 0):
                        found.append((
                            y_at[dy] * (2 * ZS) + pz * 2 + core_at[dc],
                            pz * (2 * ys) + y_at[dy] * 2 + core_at[dc],
                        ))
        return found

    everyone = peers([lax.rem(z + i, ZS) for i in (4, 3, 5, 2, 6, 1, 7, 0)], True)
    near = peers([z_half * 4 + lax.rem(z_low + i, 4) for i in (2, 1, 3, 0)], True)
    far = peers([(1 - z_half) * 4 + lax.rem(z_low + i, 4) for i in (0, 1, 3, 2)], False)

    barrier = pltpu.get_barrier_semaphore()
    load_sig = pltpu.make_async_copy(sig_hbm, sig, in_sems.at[0])
    load_sig.start()
    for to, _ in everyone:
        pl.semaphore_signal(barrier, inc=1, device_id={"seq": to}, device_id_type=MESH)
    mate, other = hd + 1 - 2 * lax.rem(hd, 2), heads - 1 - hd
    opp = lax.rem(hd + 2, heads)
    for to in (mate, other):
        pl.semaphore_signal(barrier, inc=1, device_id={"head": to}, device_id_type=MESH)

    def columns(h):
        return pl.ds(pl.multiple_of(h * width, width), width)

    small = (
        (wf_hbm, wf_ref), (bf_hbm, bf_ref), (freq_hbm, freq_ref), (wm_hbm, wm_ref), (wl_hbm, wl_ref),
        (rate_hbm, rate_ref), (skip_hbm, skip_ref), (feat_hbm, feat_ref),
        (gate_hbm, gate), (w_hbm, w_own),
    )
    loads = [pltpu.make_async_copy(src, dst, in_sems.at[i + 1]) for i, (src, dst) in enumerate(small)]
    for load in loads:
        load.start()

    load_sig.wait()
    xt = sig[...].astype(jnp.float32).T
    for h in range(2):
        piece = xt[h * (width // 2) : (h + 1) * (width // 2)].reshape(n // 2, 8, rows)
        one, two = swap_halves(piece[:, :, :LANES], piece[:, :, LANES:])
        xsend[h] = jnp.stack([one, two], 1).reshape(n, 8, LANES).astype(jnp.bfloat16)

    pl.semaphore_wait(barrier, n - 1 + 2)

    half = pl.ds(pl.multiple_of(core * (width // 2), width // 2), width // 2)
    fetches = [
        pltpu.make_async_remote_copy(
            src_ref=w_hbm.at[half, columns(of)], dst_ref=w_near.at[i, half], send_sem=ws_sems.at[i],
            recv_sem=wr_sems.at[i], device_id={"head": to}, device_id_type=MESH,
        )
        for i, (of, to) in enumerate(((mate, mate), (opp, mate), (other, other), (opp, other)))
    ]
    for i in (0, 2):
        fetches[i].start()

    for h in range(2):
        for to, slot in everyone:
            pltpu.make_async_remote_copy(
                src_ref=xsend.at[h, slot], dst_ref=xrecv.at[h, me], send_sem=xs_sems.at[h],
                recv_sem=xr_sems.at[h], device_id={"seq": to}, device_id_type=MESH,
            ).start()
    for h in range(2):
        xrecv[h, pl.ds(me, 1)] = xsend[h, pl.ds(own_group, 1)]

    for load in loads[:8]:
        load.wait()
    pad = jnp.zeros((LANES - wl_ref.shape[0] - 2, width), jnp.float32)
    stacked = jnp.concatenate([wl_ref[...], rate_ref[...], skip_ref[...], pad], 0)
    params[...] = stacked.T
    pair = own_group - core
    lower, upper = [
        params[pl.ds(pl.multiple_of(pair * part_group + h * (width // 2), 8), 8), :] for h in range(2)
    ]
    first_rows = lax.broadcasted_iota(jnp.int32, (8, LANES), 0) < 4
    even = jnp.where(first_rows, lower, pltpu.roll(upper, 4, 0))
    odd = jnp.where(first_rows, pltpu.roll(lower, 4, 0), upper)
    own = jnp.where(core == 0, even, odd)
    hidden = wl_ref.shape[0]
    rate = own[:, hidden : hidden + 1]
    freq = freq_ref[...]
    wfb = jnp.concatenate(
        [wf_ref[...], bf_ref[...], jnp.zeros((40 - wf_ref.shape[0] - 1, hidden), jnp.float32)], 0
    ) * freq
    wm = wm_ref[...] * freq
    step = 512
    for j in range(K // step):
        here = slice(j * step, (j + 1) * step)
        first = sine(dot_t(wfb, feat_ref[:, here]))
        second = sine(dot_t(wm, first))
        raw = jnp.dot(
            own[:, :hidden], second, precision=lax.Precision.HIGHEST, preferred_element_type=jnp.float32
        )
        t = (lax.broadcasted_iota(jnp.int32, (group, step), 1) + j * step).astype(jnp.float32)
        taps_here = (raw * jnp.exp(-rate * t)).astype(jnp.bfloat16).astype(jnp.float32)
        h_ref[:, :, here] = jnp.broadcast_to(taps_here[:, None], (group, 8, step))
    skip_col = jnp.broadcast_to(own[:, hidden + 1 : hidden + 2], (group, LANES))
    skips[...] = jnp.broadcast_to(skip_col[:, None], (group, 8, LANES))

    causal = lax.broadcasted_iota(jnp.int32, (LANES, LANES), 1) >= lax.broadcasted_iota(
        jnp.int32, (LANES, LANES), 0
    )

    def build(c, carry):
        last = jnp.zeros((LANES, LANES), jnp.float32)
        for m in range(taps + 1):
            if m < taps:
                line = rows_of(h_ref[c, :, m * LANES : (m + 1) * LANES], LANES)
                rolled = pltpu.roll(line, 0, 1, stride=1, stride_axis=0)
            else:
                rolled = jnp.zeros((LANES, LANES), jnp.float32)
            toep[c, m * LANES : (m + 1) * LANES, :] = jnp.where(causal, rolled, last).astype(jnp.bfloat16)
            last = rolled
        return carry

    lax.fori_loop(0, group, build, 0)
    for i in (1, 3):
        fetches[i].start()

    every = pl.ds(0, n - 1)
    front = taps * part_group
    partner = me + 1 - 2 * core

    def exchanged(h):
        return pltpu.make_async_remote_copy(
            src_ref=xsend.at[h, every], dst_ref=xrecv.at[h, every], send_sem=xs_sems.at[h],
            recv_sem=xr_sems.at[h], device_id={"seq": partner}, device_id_type=MESH,
        )

    for h in range(2):
        exchanged(h).wait_recv()
        xf[h, :front, :] = jnp.zeros((front, LANES), jnp.float32)
        xf[h, front:, :] = xrecv[h].astype(jnp.float32).reshape(blocks * part_group, LANES)

        def convolve(c, carry, h=h):
            pieces = [
                xf[h, pl.ds((taps - m) * part_group + c, blocks, stride=part_group), :] for m in range(taps + 1)
            ]
            lhs = jnp.concatenate([p.astype(jnp.bfloat16) for p in pieces], 1)
            channel = c + h * part_group
            conv = jnp.dot(lhs, toep[channel], preferred_element_type=jnp.float32)
            yf[h, pl.ds(c, blocks, stride=part_group), :] = conv + rows_of(skips[channel], blocks) * pieces[0]
            return carry

        lax.fori_loop(0, part_group, convolve, 0, unroll=True)
        ysend[h] = yf[h].reshape(n, 8, LANES).astype(jnp.bfloat16)
        for to, _ in far + near:
            pltpu.make_async_remote_copy(
                src_ref=ysend.at[h, to], dst_ref=yrecv.at[h, own_group], send_sem=ys_sems.at[h],
                recv_sem=yr_sems.at[h, z_half], device_id={"seq": to}, device_id_type=MESH,
            ).start()
        yrecv[h, pl.ds(own_group, 1)] = ysend[h, pl.ds(me, 1)]

    def onward(i, ref):
        return pltpu.make_async_remote_copy(
            src_ref=ref, dst_ref=ref, send_sem=fs_sems.at[i], recv_sem=fr_sems.at[i],
            device_id={"seq": partner}, device_id_type=MESH,
        )

    passes = [onward(i, w_near.at[i, half]) for i in range(4)]
    for i in (0, 2):
        fetches[i].wait_recv()
        passes[i].start()
    loads[8].wait()

    sides = (pl.ds(0, rows // 2), pl.ds(rows // 2, rows // 2))
    neighbours = (mate, other)

    def give(side, b, chunks):
        return pltpu.make_async_remote_copy(
            src_ref=mixed.at[0, chunks, sides[side]], dst_ref=mixed.at[1 + side, chunks, sides[side]],
            send_sem=gs_sems.at[side, b], recv_sem=gr_sems.at[side, b],
            device_id={"head": neighbours[side]}, device_id_type=MESH,
        )

    order = [(h, z_half if g == 0 else 1 - z_half, g) for h in range(2) for g in range(2)]
    for b, (h, zs, g) in enumerate(order):
        p = h * 2 + zs
        some = pl.ds(0, per_chunk if g else per_chunk - 1)
        pltpu.make_async_remote_copy(
            src_ref=ysend.at[h, some], dst_ref=yrecv.at[h, some], send_sem=ys_sems.at[h],
            recv_sem=yr_sems.at[h, zs], device_id={"seq": partner}, device_id_type=MESH,
        ).wait_recv()
        v = yrecv[h, pl.ds(pl.multiple_of(zs * per_chunk, per_chunk), per_chunk)].astype(jnp.float32)
        v = v.reshape(per_chunk // 2, 2, 8, LANES)
        channels = pl.ds(pl.multiple_of(p * LANES, LANES), LANES)
        for side, piece in enumerate(swap_halves(v[:, 0], v[:, 1])):
            here = slice(side * LANES, (side + 1) * LANES)
            vt = piece.reshape(LANES, LANES).T
            mixed[0, p, here, :] = (gate[here, channels].astype(jnp.float32) * vt).astype(jnp.bfloat16)
        for side in range(2):
            give(side, h, pl.ds(p, 1)).start()
        if b == 0:
            for i in (1, 3):
                fetches[i].wait_recv()
                passes[i].start()

    def product(slot, side, h, weights, cols):
        lhs = jnp.concatenate([mixed[slot, 2 * h + i, side * LANES : (side + 1) * LANES] for i in range(2)], 1)
        depth = slice(h * (width // 2), (h + 1) * (width // 2))
        return jnp.dot(lhs, weights[depth, cols], preferred_element_type=jnp.float32)

    gifts = [[give(side, h, pl.ds(2 * h, 2)) for h in range(2)] for side in range(2)]
    loads[9].wait()
    for weights in passes:
        weights.wait_recv()
    whole = slice(0, width)
    for side in range(2):
        gifts[side][0].wait_recv()
        theirs = columns(neighbours[1 - side])
        part[side] = (
            product(0, side, 0, w_own, theirs) + product(0, side, 1, w_own, theirs)
            + product(1 + side, side, 0, w_near.at[2 * side + 1], whole)
        )
    sums = []
    for side in range(2):
        gifts[side][1].wait_recv()
        psend[side] = (part[side] + product(1 + side, side, 1, w_near.at[2 * side + 1], whole)).astype(jnp.bfloat16)
        sums.append(pltpu.make_async_remote_copy(
            src_ref=psend.at[side], dst_ref=precv.at[side], send_sem=ps_sems.at[side], recv_sem=pr_sems.at[side],
            device_id={"head": neighbours[1 - side]}, device_id_type=MESH,
        ))
        sums[side].start()
    for side in range(2):
        part[side] = sum(
            product(0, side, h, w_own, columns(hd)) + product(1 + side, side, h, w_near.at[2 * side], whole)
            for h in range(2)
        )
    for side in range(2):
        sums[side].wait_recv()
        out_ref[side * LANES : (side + 1) * LANES, :] = (
            part[side] + precv[side].astype(jnp.float32)
        ).astype(jnp.bfloat16)

    for copies in (*gifts, sums, passes, fetches):
        for copy in copies:
            copy.wait_send()
    for h in range(2):
        exchanged(h).wait_send()
        pltpu.make_async_remote_copy(
            src_ref=ysend.at[h, every], dst_ref=yrecv.at[h, every], send_sem=ys_sems.at[h],
            recv_sem=yr_sems.at[h, 0], device_id={"seq": partner}, device_id_type=MESH,
        ).wait_send()


def local(signal, gate, skip, w_first, b_first, freq, w_mid, w_last, rate, out_w):
    n, heads = lax.axis_size("seq"), lax.axis_size("head")
    rows, width = signal.shape
    group = width // n
    bf16, f32 = jnp.bfloat16, jnp.float32
    vmem = pl.BlockSpec(memory_space=pltpu.VMEM)
    hbm = pl.BlockSpec(memory_space=pl.ANY)
    dma = pltpu.SemaphoreType.DMA
    operands = (
        signal, gate, skip[None], w_first, b_first[None], freq[None], w_mid, w_last, rate[None], out_w,
        jnp.asarray(features()),
    )
    return pl.pallas_call(
        functools.partial(kernel, n, heads),
        out_shape=pltpu.VMEM((rows, width), bf16),
        in_specs=[hbm] * 11,
        out_specs=vmem,
        scratch_shapes=[
            pltpu.VMEM((rows, width), bf16),
            pltpu.VMEM((rows, width), bf16),
            *[pltpu.VMEM(a.shape, a.dtype) for a in operands[2:9]],
            pltpu.VMEM(operands[10].shape, f32),
            pltpu.VMEM(out_w.shape, bf16),
            pltpu.VMEM((4, width, width), bf16),
            pltpu.VMEM((2, n, group, LANES), bf16),
            pltpu.VMEM((2, n, group, LANES), bf16),
            pltpu.VMEM((2, (2 * n + K // LANES) * group // 2, LANES), f32),
            pltpu.VMEM((width, LANES), f32),
            pltpu.VMEM((group, 8, K), f32),
            pltpu.VMEM((group, 8, LANES), f32),
            pltpu.VMEM((group, K + LANES, LANES), bf16),
            pltpu.VMEM((2, n * group, LANES), f32),
            pltpu.VMEM((2, n, group, LANES), bf16),
            pltpu.VMEM((2, n, group, LANES), bf16),
            pltpu.VMEM((3, width // LANES, rows, LANES), bf16),
            pltpu.VMEM((2, rows // 2, width), f32),
            pltpu.VMEM((2, rows // 2, width), bf16),
            pltpu.VMEM((2, rows // 2, width), bf16),
            dma((11,)), dma((2,)), dma((2,)), dma((2,)), dma((2, 2)), dma((4,)), dma((4,)),
            dma((4,)), dma((4,)), dma((2, 2)), dma((2, 2)), dma((2,)), dma((2,)),
        ],
        compiler_params=pltpu.CompilerParams(collective_id=0, has_side_effects=True),
    )(*operands)


def solution(mesh):
    placed = (
        P("seq", "head"),
        P("seq", "head"),
        P("head"),
        P(),
        P(),
        P(),
        P(),
        P(None, "head"),
        P("head"),
        P("head", None),
    )
    return jax.shard_map(
        local, mesh=mesh, in_specs=placed, out_specs=P("seq", "head"), check_vma=False
    )
```

```python
import functools
import math

import jax
import jax.numpy as jnp
import numpy as np
from jax import lax
from jax.experimental import pallas as pl
from jax.experimental.pallas import tpu as pltpu
from jax.sharding import PartitionSpec as P

K = 2048
BANDS = 16
LANES = 128
ZS = 8
MESH = pl.DeviceIdType.MESH


def features():
    t = np.arange(K, dtype=np.float64)
    bands = np.arange(1, BANDS + 1, dtype=np.float64)
    angles = 2.0 * math.pi * t[None, :] * bands[:, None] / K
    rows = np.concatenate([t[None] / K, np.cos(angles), np.sin(angles), np.ones((1, K))], 0)
    rows = np.concatenate([rows, np.zeros((40 - rows.shape[0], K))], 0)
    return rows.astype(np.float32)


def sine(x):
    turns = jnp.round(x * (1.0 / math.pi))
    r = (x - turns * 3.140625) - turns * (math.pi - 3.140625)
    s = r * r
    p = -1.0 / 39916800.0
    for c in (1.0 / 362880.0, -1.0 / 5040.0, 1.0 / 120.0, -1.0 / 6.0):
        p = p * s + c
    v = r + r * s * p
    odd = jnp.bitwise_and(turns.astype(jnp.int32), 1)
    return jnp.where(odd == 1, -v, v)


def rows_of(tile, count):
    copies = jnp.broadcast_to(tile[None], (count // tile.shape[0], *tile.shape))
    return copies.reshape(count, tile.shape[1])


def dot_t(a, b):
    return lax.dot_general(
        a, b, (((0,), (0,)), ((), ())),
        precision=lax.Precision.HIGHEST, preferred_element_type=jnp.float32,
    )


def swap_halves(one, two):
    upper = lax.broadcasted_iota(jnp.int32, one.shape, 1) < 4
    moved_one, moved_two = pltpu.roll(one, 4, 1), pltpu.roll(two, 4, 1)
    return jnp.where(upper, one, moved_two), jnp.where(upper, moved_one, two)


def kernel(
    n, heads, sig_hbm, gate_hbm, skip_hbm, wf_hbm, bf_hbm, freq_hbm, wm_hbm, wl_hbm, rate_hbm, w_hbm, feat_hbm,
    out_ref,
    sig, gate, skip_ref, wf_ref, bf_ref, freq_ref, wm_ref, wl_ref, rate_ref, feat_ref,
    w_own, w_near, xsend, xrecv, xf, params, h_ref, skips, toep, yf, ysend, yrecv, mixed, part, psend, precv,
    in_sems, xs_sems, xr_sems, ys_sems, yr_sems, ws_sems, wr_sems, fs_sems, fr_sems, gs_sems, gr_sems, ps_sems, pr_sems,
):
    me = lax.axis_index("seq")
    hd = lax.axis_index("head")
    rows, width = sig.shape
    group = width // n
    part_group = group // 2
    per_chunk = n // 2
    taps = K // LANES
    blocks = 2 * n

    ys = n // (2 * ZS)
    y, z, core = me // (2 * ZS), lax.rem(me // 2, ZS), lax.rem(me, 2)
    z_half, z_low = z // 4, lax.rem(z, 4)
    own_group = z * (2 * ys) + y * 2 + core
    y_at = [lax.rem(y + i, ys) for i in range(ys)]
    core_at = [core, 1 - core]

    def peers(z_list, own_first):
        found = []
        for i, pz in enumerate(z_list):
            for dy in (2, 1, 3, 0):
                for dc in (1, 0):
                    if not (own_first and i == len(z_list) - 1 and dy == 0 and dc == 0):
                        found.append((
                            y_at[dy] * (2 * ZS) + pz * 2 + core_at[dc],
                            pz * (2 * ys) + y_at[dy] * 2 + core_at[dc],
                        ))
        return found

    everyone = peers([lax.rem(z + i, ZS) for i in (4, 3, 5, 2, 6, 1, 7, 0)], True)
    near = peers([z_half * 4 + lax.rem(z_low + i, 4) for i in (2, 1, 3, 0)], True)
    far = peers([(1 - z_half) * 4 + lax.rem(z_low + i, 4) for i in (0, 1, 3, 2)], False)

    barrier = pltpu.get_barrier_semaphore()
    load_sig = pltpu.make_async_copy(sig_hbm, sig, in_sems.at[0])
    load_sig.start()
    for to, _ in everyone:
        pl.semaphore_signal(barrier, inc=1, device_id={"seq": to}, device_id_type=MESH)
    mate, other = hd + 1 - 2 * lax.rem(hd, 2), heads - 1 - hd
    opp = lax.rem(hd + 2, heads)
    for to in (mate, other):
        pl.semaphore_signal(barrier, inc=1, device_id={"head": to}, device_id_type=MESH)

    def columns(h):
        return pl.ds(pl.multiple_of(h * width, width), width)

    small = (
        (wf_hbm, wf_ref), (bf_hbm, bf_ref), (freq_hbm, freq_ref), (wm_hbm, wm_ref), (wl_hbm, wl_ref),
        (rate_hbm, rate_ref), (skip_hbm, skip_ref), (feat_hbm, feat_ref),
        (gate_hbm, gate), (w_hbm, w_own),
    )
    loads = [pltpu.make_async_copy(src, dst, in_sems.at[i + 1]) for i, (src, dst) in enumerate(small)]
    for load in loads:
        load.start()

    load_sig.wait()
    xt = sig[...].astype(jnp.float32).T
    for h in range(2):
        piece = xt[h * (width // 2) : (h + 1) * (width // 2)].reshape(n // 2, 8, rows)
        one, two = swap_halves(piece[:, :, :LANES], piece[:, :, LANES:])
        xsend[h] = jnp.stack([one, two], 1).reshape(n, 8, LANES).astype(jnp.bfloat16)

    pl.semaphore_wait(barrier, n - 1 + 2)

    half = pl.ds(pl.multiple_of(core * (width // 2), width // 2), width // 2)
    fetches = [
        pltpu.make_async_remote_copy(
            src_ref=w_hbm.at[half, columns(of)], dst_ref=w_near.at[i, half], send_sem=ws_sems.at[i],
            recv_sem=wr_sems.at[i], device_id={"head": to}, device_id_type=MESH,
        )
        for i, (of, to) in enumerate(((mate, mate), (opp, mate), (other, other), (opp, other)))
    ]
    for i in (0, 2):
        fetches[i].start()

    def send_x(h):
        for to, slot in everyone:
            pltpu.make_async_remote_copy(
                src_ref=xsend.at[h, slot], dst_ref=xrecv.at[h, me], send_sem=xs_sems.at[h],
                recv_sem=xr_sems.at[h], device_id={"seq": to}, device_id_type=MESH,
            ).start()
        xrecv[h, pl.ds(me, 1)] = xsend[h, pl.ds(own_group, 1)]

    send_x(0)

    for load in loads[:8]:
        load.wait()
    pad = jnp.zeros((LANES - wl_ref.shape[0] - 2, width), jnp.float32)
    stacked = jnp.concatenate([wl_ref[...], rate_ref[...], skip_ref[...], pad], 0)
    params[...] = stacked.T
    pair = own_group - core
    lower, upper = [
        params[pl.ds(pl.multiple_of(pair * part_group + h * (width // 2), 8), 8), :] for h in range(2)
    ]
    first_rows = lax.broadcasted_iota(jnp.int32, (8, LANES), 0) < 4
    even = jnp.where(first_rows, lower, pltpu.roll(upper, 4, 0))
    odd = jnp.where(first_rows, pltpu.roll(lower, 4, 0), upper)
    own = jnp.where(core == 0, even, odd)
    hidden = wl_ref.shape[0]
    rate = own[:, hidden : hidden + 1]
    freq = freq_ref[...]
    wfb = jnp.concatenate(
        [wf_ref[...], bf_ref[...], jnp.zeros((40 - wf_ref.shape[0] - 1, hidden), jnp.float32)], 0
    ) * freq
    wm = wm_ref[...] * freq
    step = 512
    for j in range(K // step):
        here = slice(j * step, (j + 1) * step)
        if j == 0:
            send_x(1)
        first = sine(dot_t(wfb, feat_ref[:, here]))
        second = sine(dot_t(wm, first))
        raw = jnp.dot(
            own[:, :hidden], second, precision=lax.Precision.HIGHEST, preferred_element_type=jnp.float32
        )
        t = (lax.broadcasted_iota(jnp.int32, (group, step), 1) + j * step).astype(jnp.float32)
        taps_here = (raw * jnp.exp(-rate * t)).astype(jnp.bfloat16).astype(jnp.float32)
        h_ref[:, :, here] = jnp.broadcast_to(taps_here[:, None], (group, 8, step))
    skip_col = jnp.broadcast_to(own[:, hidden + 1 : hidden + 2], (group, LANES))
    skips[...] = jnp.broadcast_to(skip_col[:, None], (group, 8, LANES))

    causal = lax.broadcasted_iota(jnp.int32, (LANES, LANES), 1) >= lax.broadcasted_iota(
        jnp.int32, (LANES, LANES), 0
    )

    def build(c, carry):
        last = jnp.zeros((LANES, LANES), jnp.float32)
        for m in range(taps + 1):
            if m < taps:
                line = rows_of(h_ref[c, :, m * LANES : (m + 1) * LANES], LANES)
                rolled = pltpu.roll(line, 0, 1, stride=1, stride_axis=0)
            else:
                rolled = jnp.zeros((LANES, LANES), jnp.float32)
            toep[c, m * LANES : (m + 1) * LANES, :] = jnp.where(causal, rolled, last).astype(jnp.bfloat16)
            last = rolled
        return carry

    lax.fori_loop(0, group, build, 0)
    for i in (1, 3):
        fetches[i].start()

    every = pl.ds(0, n - 1)
    front = taps * part_group
    partner = me + 1 - 2 * core

    def exchanged(h):
        return pltpu.make_async_remote_copy(
            src_ref=xsend.at[h, every], dst_ref=xrecv.at[h, every], send_sem=xs_sems.at[h],
            recv_sem=xr_sems.at[h], device_id={"seq": partner}, device_id_type=MESH,
        )

    for h in range(2):
        exchanged(h).wait_recv()
        xf[h, :front, :] = jnp.zeros((front, LANES), jnp.float32)
        xf[h, front:, :] = xrecv[h].astype(jnp.float32).reshape(blocks * part_group, LANES)

        def convolve(c, carry, h=h):
            pieces = [
                xf[h, pl.ds((taps - m) * part_group + c, blocks, stride=part_group), :] for m in range(taps + 1)
            ]
            lhs = jnp.concatenate([p.astype(jnp.bfloat16) for p in pieces], 1)
            channel = c + h * part_group
            conv = jnp.dot(lhs, toep[channel], preferred_element_type=jnp.float32)
            yf[h, pl.ds(c, blocks, stride=part_group), :] = conv + rows_of(skips[channel], blocks) * pieces[0]
            return carry

        lax.fori_loop(0, part_group, convolve, 0, unroll=True)
        ysend[h] = yf[h].reshape(n, 8, LANES).astype(jnp.bfloat16)
        for to, _ in far + near:
            pltpu.make_async_remote_copy(
                src_ref=ysend.at[h, to], dst_ref=yrecv.at[h, own_group], send_sem=ys_sems.at[h],
                recv_sem=yr_sems.at[h, z_half], device_id={"seq": to}, device_id_type=MESH,
            ).start()
        yrecv[h, pl.ds(own_group, 1)] = ysend[h, pl.ds(me, 1)]

    def onward(i, ref):
        return pltpu.make_async_remote_copy(
            src_ref=ref, dst_ref=ref, send_sem=fs_sems.at[i], recv_sem=fr_sems.at[i],
            device_id={"seq": partner}, device_id_type=MESH,
        )

    passes = [onward(i, w_near.at[i, half]) for i in range(4)]
    for i in (0, 2):
        fetches[i].wait_recv()
        passes[i].start()
    loads[8].wait()

    sides = (pl.ds(0, rows // 2), pl.ds(rows // 2, rows // 2))
    neighbours = (mate, other)

    def give(side, b, chunks):
        return pltpu.make_async_remote_copy(
            src_ref=mixed.at[0, chunks, sides[side]], dst_ref=mixed.at[1 + side, chunks, sides[side]],
            send_sem=gs_sems.at[side, b], recv_sem=gr_sems.at[side, b],
            device_id={"head": neighbours[side]}, device_id_type=MESH,
        )

    order = [(h, z_half if g == 0 else 1 - z_half, g) for h in range(2) for g in range(2)]
    for b, (h, zs, g) in enumerate(order):
        p = h * 2 + zs
        some = pl.ds(0, per_chunk if g else per_chunk - 1)
        pltpu.make_async_remote_copy(
            src_ref=ysend.at[h, some], dst_ref=yrecv.at[h, some], send_sem=ys_sems.at[h],
            recv_sem=yr_sems.at[h, zs], device_id={"seq": partner}, device_id_type=MESH,
        ).wait_recv()
        v = yrecv[h, pl.ds(pl.multiple_of(zs * per_chunk, per_chunk), per_chunk)].astype(jnp.float32)
        v = v.reshape(per_chunk // 2, 2, 8, LANES)
        channels = pl.ds(pl.multiple_of(p * LANES, LANES), LANES)
        for side, piece in enumerate(swap_halves(v[:, 0], v[:, 1])):
            here = slice(side * LANES, (side + 1) * LANES)
            vt = piece.reshape(LANES, LANES).T
            mixed[0, p, here, :] = (gate[here, channels].astype(jnp.float32) * vt).astype(jnp.bfloat16)
        for side in range(2):
            give(side, h, pl.ds(p, 1)).start()
        if b == 0:
            for i in (1, 3):
                fetches[i].wait_recv()
                passes[i].start()

    def product(slot, side, h, weights, cols):
        lhs = jnp.concatenate([mixed[slot, 2 * h + i, side * LANES : (side + 1) * LANES] for i in range(2)], 1)
        depth = slice(h * (width // 2), (h + 1) * (width // 2))
        return jnp.dot(lhs, weights[depth, cols], preferred_element_type=jnp.float32)

    gifts = [[give(side, h, pl.ds(2 * h, 2)) for h in range(2)] for side in range(2)]
    loads[9].wait()
    for weights in passes:
        weights.wait_recv()
    whole = slice(0, width)
    for side in range(2):
        gifts[side][0].wait_recv()
        theirs = columns(neighbours[1 - side])
        part[side] = (
            product(0, side, 0, w_own, theirs) + product(0, side, 1, w_own, theirs)
            + product(1 + side, side, 0, w_near.at[2 * side + 1], whole)
        )
    sums = []
    for side in range(2):
        gifts[side][1].wait_recv()
        psend[side] = (part[side] + product(1 + side, side, 1, w_near.at[2 * side + 1], whole)).astype(jnp.bfloat16)
        sums.append(pltpu.make_async_remote_copy(
            src_ref=psend.at[side], dst_ref=precv.at[side], send_sem=ps_sems.at[side], recv_sem=pr_sems.at[side],
            device_id={"head": neighbours[1 - side]}, device_id_type=MESH,
        ))
        sums[side].start()
    for side in range(2):
        part[side] = sum(
            product(0, side, h, w_own, columns(hd)) + product(1 + side, side, h, w_near.at[2 * side], whole)
            for h in range(2)
        )
    for side in range(2):
        sums[side].wait_recv()
        out_ref[side * LANES : (side + 1) * LANES, :] = (
            part[side] + precv[side].astype(jnp.float32)
        ).astype(jnp.bfloat16)

    for copies in (*gifts, sums, passes, fetches):
        for copy in copies:
            copy.wait_send()
    for h in range(2):
        exchanged(h).wait_send()
        pltpu.make_async_remote_copy(
            src_ref=ysend.at[h, every], dst_ref=yrecv.at[h, every], send_sem=ys_sems.at[h],
            recv_sem=yr_sems.at[h, 0], device_id={"seq": partner}, device_id_type=MESH,
        ).wait_send()


def local(signal, gate, skip, w_first, b_first, freq, w_mid, w_last, rate, out_w):
    n, heads = lax.axis_size("seq"), lax.axis_size("head")
    rows, width = signal.shape
    group = width // n
    bf16, f32 = jnp.bfloat16, jnp.float32
    vmem = pl.BlockSpec(memory_space=pltpu.VMEM)
    hbm = pl.BlockSpec(memory_space=pl.ANY)
    dma = pltpu.SemaphoreType.DMA
    operands = (
        signal, gate, skip[None], w_first, b_first[None], freq[None], w_mid, w_last, rate[None], out_w,
        jnp.asarray(features()),
    )
    return pl.pallas_call(
        functools.partial(kernel, n, heads),
        out_shape=pltpu.VMEM((rows, width), bf16),
        in_specs=[hbm] * 11,
        out_specs=vmem,
        scratch_shapes=[
            pltpu.VMEM((rows, width), bf16),
            pltpu.VMEM((rows, width), bf16),
            *[pltpu.VMEM(a.shape, a.dtype) for a in operands[2:9]],
            pltpu.VMEM(operands[10].shape, f32),
            pltpu.VMEM(out_w.shape, bf16),
            pltpu.VMEM((4, width, width), bf16),
            pltpu.VMEM((2, n, group, LANES), bf16),
            pltpu.VMEM((2, n, group, LANES), bf16),
            pltpu.VMEM((2, (2 * n + K // LANES) * group // 2, LANES), f32),
            pltpu.VMEM((width, LANES), f32),
            pltpu.VMEM((group, 8, K), f32),
            pltpu.VMEM((group, 8, LANES), f32),
            pltpu.VMEM((group, K + LANES, LANES), bf16),
            pltpu.VMEM((2, n * group, LANES), f32),
            pltpu.VMEM((2, n, group, LANES), bf16),
            pltpu.VMEM((2, n, group, LANES), bf16),
            pltpu.VMEM((3, width // LANES, rows, LANES), bf16),
            pltpu.VMEM((2, rows // 2, width), f32),
            pltpu.VMEM((2, rows // 2, width), bf16),
            pltpu.VMEM((2, rows // 2, width), bf16),
            dma((11,)), dma((2,)), dma((2,)), dma((2,)), dma((2, 2)), dma((4,)), dma((4,)),
            dma((4,)), dma((4,)), dma((2, 2)), dma((2, 2)), dma((2,)), dma((2,)),
        ],
        compiler_params=pltpu.CompilerParams(
            collective_id=0, has_side_effects=True
        ),
    )(*operands)


def solution(mesh):
    placed = (
        P("seq", "head"),
        P("seq", "head"),
        P("head"),
        P(),
        P(),
        P(),
        P(),
        P(None, "head"),
        P("head"),
        P("head", None),
    )
    return jax.shard_map(
        local, mesh=mesh, in_specs=placed, out_specs=P("seq", "head"), check_vma=False
    )
```
